512 devices in a mesh: member: 2 (over core), fsdp: 256 (over y, x, z).
Axes of the slice: x: 4, y: 8, z: 8, core: 2. Of those that a mesh axis runs over, the one named last changes fastest.
Arguments:
- hidden: bfloat16 [2, 512, 2048], P('member', 'fsdp'), may hold values from -60 to 60
- gain: float32 [2, 2048], P('member'), may hold values from 0.5 to 1.5
- head: bfloat16 [2, 2048, 128256], P('member', None, 'fsdp'), may hold values from -0.397747564 to 0.397747564
- labels: int32 [512], replicated, may hold values from 0 to 128255
Outputs:
- token_loss: float32 [2, 512], P('member', 'fsdp')
- head_grad: bfloat16 [2, 2048, 128256], P('member', None, 'fsdp')
- hidden_grad: bfloat16 [2, 512, 2048], P('member', 'fsdp')
The draws below stay inside these ranges and needn't reach their ends.
All inputs are finite; a program needn't handle non-finite values.
Results may differ from the reference program's by a relative error of at most 0.0049.
Values may be sent and summed in bfloat16 or wider, within the bound.
A program may use at most 64 MiB of HBM per device.

```python
import math
import jax
import jax.numpy as jnp
from jax import lax

D = 2048
VOCAB = 128256
TOKENS = 512
MEMBERS = 2


def draw_hidden(key, part):
    values = jax.random.normal(jax.random.fold_in(key, 1), (MEMBERS, TOKENS, D), jnp.float32)
    values = jnp.clip(values, -6.0, 6.0)
    return values.astype(jnp.bfloat16)


def draw_head(key, part):
    values = jax.random.normal(jax.random.fold_in(key, 3), (MEMBERS, D, VOCAB), jnp.float32)
    values = jnp.clip(values, -6.0, 6.0) * (3.0 / math.sqrt(D))
    return values.astype(jnp.bfloat16)


def set_ends(drawn, rng, low, high):
    longest = drawn.shape.index(max(drawn.shape))
    spots = []
    for shift in (0, 1):
        where = [jax.random.randint(jax.random.fold_in(rng, axis), (), 0, length) for axis, length in enumerate(drawn.shape)]
        where[longest] = (where[longest] + shift) % drawn.shape[longest]
        spots.append(tuple(where))
    return drawn.at[spots[0]].set(low).at[spots[1]].set(high)


def setup_inputs(seed: int = 0) -> dict:
    keys = jax.random.split(jax.random.key(seed), 5)
    hidden = draw_hidden(jax.random.fold_in(keys[4], 71), 0)
    gain = jnp.clip(1.0 + 0.1 * jax.random.normal(keys[1], (MEMBERS, D), jnp.float32), 0.5, 1.5)
    head = draw_head(jax.random.fold_in(keys[4], 71), 0)
    labels = set_ends(jax.random.randint(keys[3], (TOKENS,), 0, VOCAB), jax.random.fold_in(keys[3], 1), 0, VOCAB - 1).astype(jnp.int32)
    return dict(hidden=hidden, gain=gain, head=head, labels=labels)


EPS = 1e-05
BETA = 0.5

def normalize(rows, gain_row):
    values = rows.astype(jnp.float32)
    inverse = lax.rsqrt(lax.optimization_barrier(jnp.mean(values * values, axis=-1, keepdims=True)) + EPS)
    return ((values * inverse * gain_row).astype(jnp.bfloat16), inverse)

def norm_back(rows, inverse, gain_row, upstream):
    values = rows.astype(jnp.float32)
    scaled = gain_row * upstream
    inner = lax.optimization_barrier(jnp.mean(scaled * values, axis=-1, keepdims=True))
    return inverse * scaled - values * inverse ** 3 * inner

def reference(hidden, gain, head, labels):
    normed_list = []
    inverse_list = []
    logit_list = []
    total_list = []
    logprob_list = []
    for member in range(MEMBERS):
        normed, inverse = normalize(hidden[member], gain[member])
        logits = jnp.dot(normed, head[member], preferred_element_type=jnp.float32)
        row_top = lax.optimization_barrier(jnp.max(logits, axis=-1))
        row_total = lax.optimization_barrier(jnp.sum(jnp.exp(logits - row_top[:, None]), axis=-1))
        log_total = row_top + jnp.log(row_total)
        normed_list.append(normed)
        inverse_list.append(inverse)
        logit_list.append(logits)
        total_list.append(log_total)
        logprob_list.append((logits - log_total[:, None]).astype(jnp.bfloat16))
    columns = jnp.arange(VOCAB, dtype=jnp.int32)
    onehot = (labels[:, None] == columns[None, :]).astype(jnp.float32)
    losses = []
    head_grads = []
    hidden_grads = []
    for member in range(MEMBERS):
        logits = logit_list[member]
        log_total = total_list[member]
        target = jnp.exp(logprob_list[member ^ 1].astype(jnp.float32))
        student = jnp.exp(logits - log_total[:, None])
        dlogits = (((1.0 + BETA) * student - onehot - BETA * target) / TOKENS).astype(jnp.bfloat16)
        picked = lax.optimization_barrier(jnp.sum(onehot * logits, axis=-1))
        cross = lax.optimization_barrier(jnp.sum(target * (log_total[:, None] - logits), axis=-1))
        losses.append(log_total - picked + BETA * cross)
        head_grads.append(jnp.dot(normed_list[member].T, dlogits, preferred_element_type=jnp.float32).astype(jnp.bfloat16))
        upstream = jnp.dot(dlogits, head[member].T, preferred_element_type=jnp.float32)
        hidden_grads.append(norm_back(hidden[member], inverse_list[member], gain[member], upstream).astype(jnp.bfloat16))
    return (jnp.stack(losses), jnp.stack(head_grads), jnp.stack(hidden_grads))
```

```python
import functools
import math

import jax
import jax.numpy as jnp
from jax import lax
from jax.experimental import pallas as pl
from jax.experimental.pallas import tpu as pltpu
from jax.sharding import PartitionSpec as P

EPS = 1e-05
BETA = 0.5
MESH = pl.DeviceIdType.MESH
F32 = jnp.float32
BF16 = jnp.bfloat16
GRID = {256: (8, 4, 8), 8: (2, 2, 2)}
SPLIT = {2048: (384, 1024, 640), 384: (128, 128, 128)}

G1Z, G1Y, G2A, G2B, G2C, G3A, G3B, G3C = range(8)
SZ, SY, SX, TE = range(8, 12)
R1A, R1B, R1C, R2A, R2B, R2C, R3Z, R3Y = range(12, 20)
QX, QY, QZ = range(20, 23)
NEX = 23


def dot(a, b, dims):
    return lax.dot_general(a, b, (dims, ((), ())), preferred_element_type=F32)


def kernel(
    dims, parts, hid, gain, head_hbm, lab, loss, hg_hbm, hd,
    w, own, z1, y1, asz, asy, na, nc, nb, nbn, lg, tch, stz, sty, stx, ltt, labt,
    dl, dlb, ua, uc, ub, ra, rc, rb, sa2, sc2, sb2, ra2, rc2, rb2,
    s3z, s3y, r3z, r3y, qz, qy, qx, hg, ssem, rsem, csem,
):
    ny, nx, nz = dims
    fa, fc, fb = parts
    fac = fa + fc
    rows, feat = hid.shape
    tokens = lab.shape[1]
    vocab = head_hbm.shape[1]
    gz, gy = nz * rows, ny * rows

    f = lax.axis_index("fsdp")
    mem = lax.axis_index("member")
    z = lax.rem(f, nz)
    x = lax.rem(lax.div(f, nz), nx)
    y = lax.div(f, nz * nx)

    def at_z(c):
        return {"fsdp": f - z + c}

    def at_x(c):
        return {"fsdp": f + (c - x) * nz}

    def at_y(c):
        return {"fsdp": f + (c - y) * (nx * nz)}

    def copy(num, k, src, dst, dev):
        return pltpu.make_async_remote_copy(
            src_ref=src, dst_ref=dst, send_sem=ssem.at[num, k], recv_sem=rsem.at[num, k],
            device_id=dev, device_id_type=MESH,
        )

    sends = []

    class Exchange:
        def __init__(self, num, n, me, at, src, dst):
            self.n = n

            def make(k):
                c = lax.rem(me + k, n)
                return copy(num, k, src(c), dst, at(c))

            self.make = make
            sends.append(self)

        def each(self, do):
            def step(k, carry):
                do(self.make(k))
                return carry

            lax.fori_loop(1, self.n, step, 0)

        def start(self):
            self.each(lambda c: c.start())
            return self

        def arrived(self):
            self.each(lambda c: c.wait_recv())

        def sent(self):
            self.each(lambda c: c.wait_send())

    load = pltpu.make_async_copy(head_hbm, w, csem.at[0])
    load.start()

    barrier = pltpu.get_barrier_semaphore()

    def greet(dev):
        pl.semaphore_signal(barrier, inc=1, device_id=dev, device_id_type=MESH)

    def greet_all(n, me, at):
        def step(k, carry):
            greet(at(lax.rem(me + k, n)))
            return carry

        lax.fori_loop(1, n, step, 0)

    greet_all(nz, z, at_z)
    greet_all(ny, y, at_y)
    greet_all(nx, x, at_x)
    def at_x_other(c):
        return {"member": 1 - mem, "fsdp": f + (c - x) * nz}

    def greet_other(c, carry):
        greet(at_x_other(c))
        return carry

    lax.fori_loop(0, nx, greet_other, 0)

    values = hid[...].astype(F32)
    inverse = lax.rsqrt(jnp.mean(values * values, axis=-1, keepdims=True) + EPS)
    own[...] = (values * inverse * gain[...]).astype(BF16)

    pl.semaphore_wait(barrier, nz - 1 + ny - 1 + nx - 1 + nx)

    g1y = Exchange(G1Y, ny, y, at_y, lambda c: own.at[:, pl.ds(fac, fb)], y1.at[y]).start()
    g1z = Exchange(G1Z, nz, z, at_z, lambda c: own.at[:, pl.ds(0, fac)], z1.at[z]).start()

    z1[z] = own[:, :fac]
    y1[y] = own[:, fac:]
    labt[...] = jnp.broadcast_to(lab[...], (128, tokens)).T
    size = ny * gz
    lr = int(math.log2(rows))
    lz = int(math.log2(nz))
    to = lax.broadcasted_iota(jnp.int32, (size, size), 0)
    frm = lax.broadcasted_iota(jnp.int32, (size, size), 1)
    ty = to >> (lr + lz)
    tz = (to >> lr) & (nz - 1)
    perm = (frm == tz * gy + ty * rows + (to & (rows - 1))).astype(BF16)

    g1y.arrived()
    for s in range(ny):
        asy[s * rows:(s + 1) * rows, :] = y1[s].astype(F32)
    nb[x, z] = asy[...].astype(BF16)
    g2b = Exchange(G2B, nx, x, at_x, lambda c: nb.at[x, z], nb.at[x, z]).start()
    g1z.arrived()
    for s in range(nz):
        asz[s * rows:(s + 1) * rows, :] = z1[s].astype(F32)
    tile = asz[...].astype(BF16)
    na[y, x] = tile[:, :fa]
    nc[y, x] = tile[:, fa:]
    g2a = Exchange(G2A, nx, x, at_x, lambda c: na.at[y, x], na.at[y, x]).start()
    g2c = Exchange(G2C, ny, y, at_y, lambda c: nc.at[y, x], nc.at[y, x]).start()
    g2b.arrived()
    g3b = Exchange(G3B, nz, z, at_z, lambda c: nb.at[:, z], nb.at[:, z]).start()
    g2a.arrived()
    g3a = Exchange(G3A, ny, y, at_y, lambda c: na.at[y], na.at[y]).start()
    g2c.arrived()
    g3c = Exchange(G3C, nx, x, at_x, lambda c: nc.at[:, x], nc.at[:, x]).start()

    load.wait()
    g3c.arrived()
    lg[...] = dot(nc[...].reshape(tokens, fc), w[fa:fac, :], ((1,), (0,)))
    g3a.arrived()
    lg[...] += dot(na[...].reshape(tokens, fa), w[:fa, :], ((1,), (0,)))
    g3b.arrived()
    for s in range(nx):
        swap = dot(perm, nb[s].reshape(size, fb), ((1,), (0,)))
        nbn[:, s] = swap.astype(BF16).reshape(ny, gz, fb)
    lg[...] += dot(nbn[...].reshape(tokens, fb), w[fac:, :], ((1,), (0,)))
    other = copy(TE, 0, lg, tch, {"member": 1 - mem})
    other.start()

    logits = lg[...]
    columns = lax.broadcasted_iota(jnp.int32, (tokens, vocab), 1)
    top = jnp.max(logits, axis=-1, keepdims=True)
    total = jnp.sum(jnp.exp(logits - top), axis=-1, keepdims=True)
    lane = lax.broadcasted_iota(jnp.int32, (tokens, 128), 1)
    both = jnp.where(lane == 0, top, total).T
    stz[z] = both[0:2, :]

    def merged(blocks):
        best = functools.reduce(jnp.maximum, [b[0:1, :] for b in blocks])
        return best, functools.reduce(jnp.add, [b[1:2, :] * jnp.exp(b[0:1, :] - best) for b in blocks])

    sz = Exchange(SZ, nz, z, at_z, lambda c: stz.at[z], stz.at[z]).start()
    sz.arrived()
    best, total = merged([stz[s] for s in range(nz)])
    sty[y, 0:1, :] = best
    sty[y, 1:2, :] = total
    sy = Exchange(SY, ny, y, at_y, lambda c: sty.at[y], sty.at[y]).start()
    sy.arrived()
    best, total = merged([sty[s] for s in range(ny)])
    stx[mem, x, 0:1, :] = best
    stx[mem, x, 1:2, :] = total

    sx = Exchange(SX, nx, x, at_x, lambda c: stx.at[mem, x], stx.at[mem, x]).start()

    def cross_copy(k):
        c = lax.rem(x + k, nx)
        return copy(SX, nx + k, stx.at[mem, x], stx.at[mem, x], at_x_other(c))

    def cross_each(do):
        def step(k, carry):
            do(cross_copy(k))
            return carry

        lax.fori_loop(0, nx, step, 0)

    cross_each(lambda c: c.start())
    sx.arrived()
    cross_each(lambda c: c.wait_recv())
    logs = []
    for who in (mem, 1 - mem):
        best, total = merged([stx[who, s] for s in range(nx)])
        logs.append(best + jnp.log(total))
    row = lax.broadcasted_iota(jnp.int32, (128, tokens), 0)
    ltt[...] = jnp.where(row == 0, logs[0], logs[1]).T

    other.wait_recv()
    local = labt[:, 0:1] - f * vocab
    mask = local == columns
    logits = lg[...]
    log_total = ltt[:, 0:1]
    target = jnp.exp((tch[...] - ltt[:, 1:2]).astype(BF16).astype(F32))
    student = jnp.exp(logits - log_total)
    grad = ((1.0 + BETA) * student - mask.astype(F32) - BETA * target) * (1.0 / tokens)
    dl[...] = grad.astype(BF16).reshape(ny, nx, gz, vocab)
    part = jnp.sum(BETA * target * (log_total - logits) - jnp.where(mask, logits, 0.0), axis=-1, keepdims=True)
    qx[x] = jnp.broadcast_to(part, (tokens, 128)).T[0:1, :]
    q1 = Exchange(QX, nx, x, at_x, lambda c: qx.at[x], qx.at[x]).start()

    for s in range(nx):
        swap = dot(perm, dl[:, s].reshape(size, vocab), ((0,), (0,)))
        dlb[s] = swap.astype(BF16).reshape(nz, gy, vocab)
    ub[...] = dot(dlb[...].reshape(tokens, vocab), w[fac:, :], ((1,), (1,))).astype(BF16).reshape(ub.shape)
    r1b = Exchange(R1B, nz, z, at_z, lambda c: ub.at[:, c], rb.at[z]).start()
    whole = dl[...].reshape(tokens, vocab)
    ua[...] = dot(whole, w[:fa, :], ((1,), (1,))).astype(BF16).reshape(ua.shape)
    r1a = Exchange(R1A, ny, y, at_y, lambda c: ua.at[c], ra.at[y]).start()
    uc[...] = dot(whole, w[fa:fac, :], ((1,), (1,))).astype(BF16).reshape(uc.shape)
    r1c = Exchange(R1C, nx, x, at_x, lambda c: uc.at[:, c], rc.at[x]).start()

    hg[:fa, :] = dot(na[...].reshape(tokens, fa), whole, ((0,), (0,))).astype(BF16)
    hg[fa:fac, :] = dot(nc[...].reshape(tokens, fc), whole, ((0,), (0,))).astype(BF16)
    hg[fac:, :] = dot(nbn[...].reshape(tokens, fb), whole, ((0,), (0,))).astype(BF16)
    store = pltpu.make_async_copy(hg, hg_hbm, csem.at[1])
    store.start()

    q1.arrived()
    qy[y] = functools.reduce(jnp.add, [qx[s] for s in range(nx)])
    q2 = Exchange(QY, ny, y, at_y, lambda c: qy.at[y], qy.at[y]).start()
    q2.arrived()
    qz[z] = functools.reduce(jnp.add, [qy[s] for s in range(ny)])
    q3 = Exchange(QZ, nz, z, at_z, lambda c: qz.at[z], qz.at[z]).start()

    def summed(mine, arrived, me, n, index):
        def step(k, acc):
            return acc + arrived[(lax.rem(me + k, n),) + index].astype(F32)

        acc = mine.astype(F32)
        for k in range(1, n):
            acc = step(k, acc)
        return acc

    r1c.arrived()
    for s in range(ny):
        sc2[s] = summed(uc[s, x], rc, x, nx, (s,)).astype(BF16)
    r2c = Exchange(R2C, ny, y, at_y, lambda c: sc2.at[c], rc2.at[y]).start()
    r1a.arrived()
    for s in range(nx):
        sa2[s] = summed(ua[y, s], ra, y, ny, (s,)).astype(BF16)
    r2a = Exchange(R2A, nx, x, at_x, lambda c: sa2.at[c], ra2.at[x]).start()
    r1b.arrived()
    for s in range(nx):
        sb2[s] = summed(ub[s, z], rb, z, nz, (s,)).astype(BF16)
    r2b = Exchange(R2B, nx, x, at_x, lambda c: sb2.at[c], rb2.at[x]).start()

    r2c.arrived()
    asz[:, fa:] = summed(sc2[y], rc2, y, ny, ())
    r2a.arrived()
    asz[:, :fa] = summed(sa2[x], ra2, x, nx, ())
    for s in range(nz):
        s3z[s] = asz[s * rows:(s + 1) * rows, :]
    r3 = Exchange(R3Z, nz, z, at_z, lambda c: s3z.at[c], r3z.at[z]).start()
    r2b.arrived()
    asy[...] = summed(sb2[x], rb2, x, nx, ())
    for s in range(ny):
        s3y[s] = asy[s * rows:(s + 1) * rows, :]
    r4 = Exchange(R3Y, ny, y, at_y, lambda c: s3y.at[c], r3y.at[y]).start()

    q3.arrived()
    losses = functools.reduce(jnp.add, [qz[s] for s in range(nz)]) + logs[0]
    spot = lax.broadcasted_iota(jnp.int32, (1, tokens), 1)
    for i in range(rows):
        loss[:, i:i + 1] = jnp.sum(jnp.where(spot == f * rows + i, losses, 0.0), axis=-1, keepdims=True)

    r3.arrived()
    r4.arrived()
    upstream = jnp.concatenate([summed(s3z[z], r3z, z, nz, ()), summed(s3y[y], r3y, y, ny, ())], axis=-1)
    scaled = gain[...] * upstream
    inner = jnp.mean(scaled * values, axis=-1, keepdims=True)
    hd[...] = (inverse * scaled - values * (inverse * inverse * inverse) * inner).astype(BF16)

    for exchange in sends:
        exchange.sent()
    cross_each(lambda c: c.wait_send())
    other.wait_send()
    store.wait()


def body(hidden, gain, head, labels):
    rows, feat = hidden.shape[1:]
    vocab = head.shape[2]
    tokens = labels.shape[0]
    ny, nx, nz = dims = GRID[tokens // rows]
    fa, fc, fb = parts = SPLIT[feat]
    fac = fa + fc
    gz, gy = nz * rows, ny * rows
    vm = pltpu.VMEM
    loss, head_grad, hidden_grad = pl.pallas_call(
        functools.partial(kernel, dims, parts),
        out_shape=(
            jax.ShapeDtypeStruct((1, rows), F32),
            jax.ShapeDtypeStruct((feat, vocab), BF16),
            jax.ShapeDtypeStruct((rows, feat), BF16),
        ),
        in_specs=[
            pl.BlockSpec(memory_space=vm),
            pl.BlockSpec(memory_space=vm),
            pl.BlockSpec(memory_space=pl.ANY),
            pl.BlockSpec(memory_space=vm),
        ],
        out_specs=(
            pl.BlockSpec(memory_space=vm),
            pl.BlockSpec(memory_space=pl.ANY),
            pl.BlockSpec(memory_space=vm),
        ),
        scratch_shapes=[
            vm((feat, vocab), BF16),
            vm((rows, feat), BF16),
            vm((nz, rows, fac), BF16),
            vm((ny, rows, fb), BF16),
            vm((gz, fac), F32),
            vm((gy, fb), F32),
            vm((ny, nx, gz, fa), BF16),
            vm((ny, nx, gz, fc), BF16),
            vm((nx, nz, gy, fb), BF16),
            vm((ny, nx, gz, fb), BF16),
            vm((tokens, vocab), F32),
            vm((tokens, vocab), F32),
            vm((nz, 2, tokens), F32),
            vm((ny, 2, tokens), F32),
            vm((2, nx, 2, tokens), F32),
            vm((tokens, 128), F32),
            vm((tokens, 128), jnp.int32),
            vm((ny, nx, gz, vocab), BF16),
            vm((nx, nz, gy, vocab), BF16),
            vm((ny, nx, gz, fa), BF16),
            vm((ny, nx, gz, fc), BF16),
            vm((nx, nz, gy, fb), BF16),
            vm((ny, nx, gz, fa), BF16),
            vm((nx, ny, gz, fc), BF16),
            vm((nz, nx, gy, fb), BF16),
            vm((nx, gz, fa), BF16),
            vm((ny, gz, fc), BF16),
            vm((nx, gy, fb), BF16),
            vm((nx, gz, fa), BF16),
            vm((ny, gz, fc), BF16),
            vm((nx, gy, fb), BF16),
            vm((nz, rows, fac), F32),
            vm((ny, rows, fb), F32),
            vm((nz, rows, fac), F32),
            vm((ny, rows, fb), F32),
            vm((nz, 1, tokens), F32),
            vm((ny, 1, tokens), F32),
            vm((nx, 1, tokens), F32),
            vm((feat, vocab), BF16),
            pltpu.SemaphoreType.DMA((NEX, 8)),
            pltpu.SemaphoreType.DMA((NEX, 8)),
            pltpu.SemaphoreType.DMA((2,)),
        ],
        compiler_params=pltpu.CompilerParams(collective_id=0, has_side_effects=True, vmem_limit_bytes=60 * 2**20),
        name="head_step",
    )(hidden[0], gain, head[0], labels.reshape(1, tokens))
    return loss, head_grad[None], hidden_grad[None]


def solution(mesh):
    in_specs = (P("member", "fsdp", None), P("member", None), P("member", None, "fsdp"), P())
    out_specs = (P("member", "fsdp"), P("member", None, "fsdp"), P("member", "fsdp", None))
    return jax.shard_map(body, mesh=mesh, in_specs=in_specs, out_specs=out_specs, check_vma=False)
```

```python
import functools
import math

import jax
import jax.numpy as jnp
from jax import lax
from jax.experimental import pallas as pl
from jax.experimental.pallas import tpu as pltpu
from jax.sharding import PartitionSpec as P

EPS = 1e-05
BETA = 0.5
MESH = pl.DeviceIdType.MESH
F32 = jnp.float32
BF16 = jnp.bfloat16
GRID = {256: (8, 4, 8), 8: (2, 2, 2), 16: (4, 2, 2), 32: (8, 2, 2)}
SPLIT = {2048: (640, 512, 896), 384: (128, 128, 128)}

NAMES = [
    "G1Z", "G1Y", "G2A", "G2B", "G2C", "G3C", "SZ", "SY", "SX", "TE", "R1C", "R2A", "R2B", "R2C", "R3Z", "R3Y",
    "QX", "QY", "QZ", "GA", "GB", "RA", "RB",
]
NUM = {name: i for i, name in enumerate(NAMES)}
RINGS = {name: i for i, name in enumerate(["GA", "GB", "RA", "RB"])}
TRACE = False


def dot(a, b, dims):
    return lax.dot_general(a, b, (dims, ((), ())), preferred_element_type=F32)


def kernel(
    dims, parts, hid_in, gain_in, head_hbm, lab_in, loss, hg, hd,
    w, own, z1, y1, asz, asy, na, nc, nb, nbn, lg, tch, stz, sty, stx, ltt, labt,
    dl, dlb, ua, uc, ub, pa, pb, ra, rc, rb, sa2, sc2, sb2, ra2, rc2, rb2,
    s3z, s3y, r3z, r3y, qz, qy, qx, ssem, rsem, gsem, xsem, csem, hid, gain, lab,
):
    ny, nx, nz = dims
    fa, fc, fb = parts
    fac = fa + fc
    rows, feat = hid.shape
    tokens = lab.shape[1]
    vocab = head_hbm.shape[0]
    gz, gy = nz * rows, ny * rows

    f = lax.axis_index("fsdp")
    mem = lax.axis_index("member")
    z = lax.rem(f, nz)
    x = lax.rem(lax.div(f, nz), nx)
    y = lax.div(f, nz * nx)

    def at_z(c):
        return {"fsdp": f - z + c}

    def at_x(c):
        return {"fsdp": f + (c - x) * nz}

    def at_y(c):
        return {"fsdp": f + (c - y) * (nx * nz)}

    def copy(name, src, dst, dev, slot=None, sems=None):
        num = NUM[name]
        arrive = rsem.at[num] if slot is None else (gsem.at[RINGS[name], slot] if sems is None else sems.at[slot])
        return pltpu.make_async_remote_copy(
            src_ref=src, dst_ref=dst, send_sem=ssem.at[num], recv_sem=arrive, device_id=dev, device_id_type=MESH
        )

    sends = []
    near = sorted(range(nx), key=lambda k: min(k, nx - k))
    upward = near[0::2]
    along = [lax.rem(x + k, nx) for k in range(nx)]

    class Exchange:
        def __init__(self, name, n, me, at, src, dst, many):
            self.n, self.me, self.at = n, me, at
            self.make = lambda c: copy(name, src(c), dst, at(c))
            self.all = copy(name, many, many, at(lax.rem(me + 1, n)))
            sends.append(self.all)

        def start(self):
            def step(k, carry):
                self.make(lax.rem(self.me + k, self.n)).start()
                return carry

            lax.fori_loop(1, self.n, step, 0)
            return self

        def arrived(self):
            self.all.wait_recv()

    class Ring:
        def __init__(self, name, n, me, at, many):
            self.name, self.n, self.me, self.at = name, n, me, at
            self.half = n // 2
            self.pending = set()
            sends.append(copy(name, many, many, at(lax.rem(me + 1, n))))

        def other(self, way, steps):
            return lax.rem(self.me + (steps if way == 0 else self.n - steps), self.n)

        def reaches(self, way, d, k):
            return d < self.half or (d == self.half and (k in upward) == (way == 0))

        def slot(self, way, d, k):
            return (way * self.half + d - 1) * nx + k

        def send(self, way, d, k, hops, src, dst):
            copy(self.name, src, dst, self.at(self.other(way, hops)), self.slot(way, d, k)).start()
            self.pending.add((way, d, k))

        def arrived(self, way, d, k, ref):
            self.pending.remove((way, d, k))
            copy(self.name, ref, ref, self.at(self.other(way, 1)), self.slot(way, d, k)).wait_recv()

    scope = []

    def stage(name):
        if TRACE:
            if scope:
                scope.pop().__exit__(None, None, None)
            if name:
                scope.append(jax.named_scope(name))
                scope[0].__enter__()

    stage("greet")
    loads = [
        pltpu.make_async_copy(src, dst, csem.at[i])
        for i, (src, dst) in enumerate([(hid_in, hid), (gain_in, gain), (lab_in, lab), (head_hbm, w)])
    ]
    for load in loads:
        load.start()

    barrier = pltpu.get_barrier_semaphore()

    def greet(dev):
        pl.semaphore_signal(barrier, inc=1, device_id=dev, device_id_type=MESH)

    def greet_all(n, me, at):
        def step(k, carry):
            greet(at(lax.rem(me + k, n)))
            return carry

        lax.fori_loop(1, n, step, 0)

    greet_all(nz, z, at_z)
    greet_all(ny, y, at_y)
    greet_all(nx, x, at_x)
    def at_x_other(c):
        return {"member": 1 - mem, "fsdp": f + (c - x) * nz}

    def greet_other(c, carry):
        greet(at_x_other(c))
        return carry

    lax.fori_loop(0, nx, greet_other, 0)

    loads[0].wait()
    loads[1].wait()
    values = hid[...].astype(F32)
    inverse = lax.rsqrt(jnp.mean(values * values, axis=-1, keepdims=True) + EPS)
    own[...] = (values * inverse * gain[...]).astype(BF16)

    stage("barrier")
    pl.semaphore_wait(barrier, nz - 1 + ny - 1 + nx - 1 + nx)

    stage("g1start")
    g1y = Exchange("G1Y", ny, y, at_y, lambda c: own.at[:, pl.ds(fac, fb)], y1.at[y], y1.at[0:ny - 1]).start()
    g1z = Exchange("G1Z", nz, z, at_z, lambda c: own.at[:, pl.ds(0, fac)], z1.at[z], z1.at[0:nz - 1]).start()

    z1[z] = own[:, :fac]
    y1[y] = own[:, fac:]
    loads[2].wait()
    labt[...] = jnp.broadcast_to(lab[...], (128, tokens)).T
    size = ny * gz
    lr = int(math.log2(rows))
    lz = int(math.log2(nz))
    to = lax.broadcasted_iota(jnp.int32, (size, size), 0)
    frm = lax.broadcasted_iota(jnp.int32, (size, size), 1)
    ty = to >> (lr + lz)
    tz = (to >> lr) & (nz - 1)
    perm = (frm == tz * gy + ty * rows + (to & (rows - 1))).astype(BF16)

    stage("g1y_wait")
    g1y.arrived()
    for s in range(ny):
        asy[s * rows:(s + 1) * rows, :] = y1[s].astype(F32)
    nb[x, z] = asy[...].astype(BF16)

    def to_row(name, which, ref):
        for k in near[1:]:
            copy(name, ref, ref, at_x(along[k]), nx - k, xsem.at[which]).start()

    def from_row(name, which, ref, k):
        copy(name, ref, ref, at_x(along[k]), k, xsem.at[which]).wait_recv()

    def block_a(b, k):
        return na.at[b, along[k]]

    def block_b(b, k):
        return nb.at[along[k], b]

    sends.append(copy("G2A", na.at[0, 0:nx - 1], na.at[0, 0:nx - 1], at_x(along[1])))
    sends.append(copy("G2B", nb.at[0:nx - 1, 0], nb.at[0:nx - 1, 0], at_x(along[1])))
    ring_a = Ring("GA", ny, y, at_y, na.at[0:ny - 1])
    ring_b = Ring("GB", nz, z, at_z, nb.at[:, 0:nz - 1])

    def hand_on(ring, block, late, k, hops=(2, 1)):
        back = 2 * late
        for way in range(2):
            if late:
                if not ring.reaches(way, 3, k):
                    continue
                ring.arrived(way, 2, k, block(ring.other(1 - way, 2), k))
            ref = block(ring.other(1 - way, back) if back else ring.me, k)
            for hop in hops:
                if ring.reaches(way, back + hop, k):
                    ring.send(way, back + hop, k, hop, ref, ref)

    def rest(ring, block):
        for way, d, k in sorted(ring.pending, key=lambda p: (p[1], near.index(p[2]))):
            ring.arrived(way, d, k, block(ring.other(1 - way, d), k))

    to_row("G2B", 1, nb.at[x, z])
    hand_on(ring_b, block_b, 0, 0)
    stage("g1z_wait")
    g1z.arrived()
    for s in range(nz):
        asz[s * rows:(s + 1) * rows, :] = z1[s].astype(F32)
    tile = asz[...].astype(BF16)
    na[y, x] = tile[:, :fa]
    to_row("G2A", 0, na.at[y, x])
    nc[y, x] = tile[:, fa:]
    g2c = Exchange("G2C", ny, y, at_y, lambda c: nc.at[y, x], nc.at[y, x], nc.at[0:ny - 1, 0]).start()
    hand_on(ring_a, block_a, 0, 0)

    def step_b(s, k):
        if s == 0:
            from_row("G2B", 1, nb.at[along[k], z], k)
        hand_on(ring_b, block_b, s, k, (2, 1) if s else (2,))

    def step_a(s, k):
        if s == 0:
            from_row("G2A", 0, na.at[y, along[k]], k)
        hand_on(ring_a, block_a, s, k, (2, 1) if s else (2,))

    def step_1(k):
        hand_on(ring_b, block_b, 0, k, (1,))
        hand_on(ring_a, block_a, 0, k, (1,))

    g3c = Exchange("G3C", nx, x, at_x, lambda c: nc.at[:, x], nc.at[:, x], nc.at[:, 0:nx - 1])

    def turn_c():
        g2c.arrived()
        g3c.start()

    events = [(4.0, "turn_c", turn_c)]
    for k in near[1:]:
        events.append((3.3 + 0.01 * k, f"n{k}", functools.partial(step_1, k)))
    for s in range(2):
        for k in range(nx):
            if (s, k) == (0, 0):
                continue
            when = 3.5 * s + 1.5 * min(k, nx - k) + 0.1 * k
            events.append((when, f"b{s}{k}", functools.partial(step_b, s, k)))
            events.append((when + 0.01, f"a{s}{k}", functools.partial(step_a, s, k)))
    for when, name, event in sorted(events, key=lambda e: e[0]):
        stage(name)
        event()

    stage("load_wait")
    loads[3].wait()
    stage("g3c_wait")
    g3c.arrived()
    stage("dot_c")
    lg[...] = dot(nc[...].reshape(tokens, fc), w[:, fa:fac], ((1,), (1,)))
    stage("g3a_wait")
    rest(ring_a, block_a)
    stage("dot_a")
    lg[...] += dot(na[...].reshape(tokens, fa), w[:, :fa], ((1,), (1,)))
    stage("g3b_wait")
    rest(ring_b, block_b)
    stage("dot_b")
    for s in range(nx):
        swap = dot(perm, nb[s].reshape(size, fb), ((1,), (0,)))
        nbn[:, s] = swap.astype(BF16).reshape(ny, gz, fb)
    lg[...] += dot(nbn[...].reshape(tokens, fb), w[:, fac:], ((1,), (1,)))
    other = copy("TE", lg, tch, {"member": 1 - mem})
    other.start()

    stage("stats")
    logits = lg[...]
    columns = lax.broadcasted_iota(jnp.int32, (tokens, vocab), 1)
    top = jnp.max(logits, axis=-1, keepdims=True)
    total = jnp.sum(jnp.exp(logits - top), axis=-1, keepdims=True)
    lane = lax.broadcasted_iota(jnp.int32, (tokens, 128), 1)
    both = jnp.where(lane == 0, top, total).T
    stz[z] = both[0:2, :]

    def merged(blocks):
        best = functools.reduce(jnp.maximum, [b[0:1, :] for b in blocks])
        return best, functools.reduce(jnp.add, [b[1:2, :] * jnp.exp(b[0:1, :] - best) for b in blocks])

    sz = Exchange("SZ", nz, z, at_z, lambda c: stz.at[z], stz.at[z], stz.at[0:nz - 1]).start()
    stage("sz_wait")
    sz.arrived()
    stage("mergez")
    best, total = merged([stz[s] for s in range(nz)])
    sty[y, 0:1, :] = best
    sty[y, 1:2, :] = total
    sy = Exchange("SY", ny, y, at_y, lambda c: sty.at[y], sty.at[y], sty.at[0:ny - 1]).start()
    stage("sy_wait")
    sy.arrived()
    stage("mergey")
    best, total = merged([sty[s] for s in range(ny)])
    mine = mem * nx + x
    stx[mine, 0:1, :] = best
    stx[mine, 1:2, :] = total

    sx = Exchange("SX", nx, x, at_x, lambda c: stx.at[mine], stx.at[mine], stx.at[0:2 * nx - 1]).start()

    def cross_step(k, carry):
        copy("SX", stx.at[mine], stx.at[mine], at_x_other(lax.rem(x + k, nx))).start()
        return carry

    lax.fori_loop(0, nx, cross_step, 0)
    stage("sx_wait")
    sx.arrived()
    stage("mergex")
    logs = []
    for who in (mem, 1 - mem):
        best, total = merged([stx[who * nx + s] for s in range(nx)])
        logs.append(best + jnp.log(total))
    row = lax.broadcasted_iota(jnp.int32, (128, tokens), 0)
    ltt[...] = jnp.where(row == 0, logs[0], logs[1]).T

    stage("teacher_wait")
    other.wait_recv()
    stage("dlogits")
    local = labt[:, 0:1] - f * vocab
    mask = local == columns
    logits = lg[...]
    log_total = ltt[:, 0:1]
    target = jnp.exp((tch[...] - ltt[:, 1:2]).astype(BF16).astype(F32))
    student = jnp.exp(logits - log_total)
    grad = ((1.0 + BETA) * student - mask.astype(F32) - BETA * target) * (1.0 / tokens)
    dl[...] = grad.astype(BF16).reshape(ny, nx, gz, vocab)
    part = jnp.sum(BETA * target * (log_total - logits) - jnp.where(mask, logits, 0.0), axis=-1, keepdims=True)
    qx[x] = jnp.broadcast_to(part, (tokens, 128)).T[0:1, :]
    q1 = Exchange("QX", nx, x, at_x, lambda c: qx.at[x], qx.at[x], qx.at[0:nx - 1]).start()

    stage("up_b")
    for s in range(nx):
        swap = dot(perm, dl[:, s].reshape(size, vocab), ((0,), (0,)))
        dlb[s] = swap.astype(BF16).reshape(nz, gy, vocab)
    back_b = Ring("RB", nz, z, at_z, pb.at[0:(nz - 1) * nx])
    back_a = Ring("RA", ny, y, at_y, pa.at[0:(ny - 1) * nx])

    def own_a(b, k):
        return ua[b, along[k]]

    def own_b(b, k):
        return ub[along[k], b]

    def send_on(ring, put, got, way, d, k, hops, acc):
        here = ring.slot(way, d, k)
        put[here] = acc.astype(BF16)
        ring.send(way, d, k, hops, put.at[here], got.at[here])

    def taken(ring, got, way, d, k, acc):
        if (way, d, k) in ring.pending:
            here = ring.slot(way, d, k)
            ring.arrived(way, d, k, got.at[here])
            acc = acc + got[here].astype(F32)
        return acc

    def far_off(ring, own_of, put, got, k):
        for d in (4, 3):
            for way in range(2):
                if ring.reaches(way, d, k):
                    send_on(ring, put, got, way, d, k, d - 2, own_of(ring.other(way, d), k))

    def next_to(ring, own_of, put, got, k):
        for way in range(2):
            if ring.reaches(way, 1, k):
                send_on(ring, put, got, way, 1, k, 1, own_of(ring.other(way, 1), k))

    def two_off(ring, own_of, put, got, k):
        for way in range(2):
            if ring.reaches(way, 2, k):
                acc = own_of(ring.other(way, 2), k)
                for d in (3, 4):
                    acc = taken(ring, got, way, d, k, acc)
                send_on(ring, put, got, way, 2, k, 2, acc)

    def ended(ring, own_of, got, k):
        acc = own_of(ring.me, k)
        for d in (1, 2):
            for way in range(2):
                acc = taken(ring, got, way, d, k, acc)
        return acc

    far = near[::-1]
    args_a = back_a, own_a, pa, ra
    args_b = back_b, own_b, pb, rb

    ub[...] = dot(dlb[...].reshape(tokens, vocab), w[:, fac:], ((1,), (0,))).reshape(ub.shape)
    for k in far:
        far_off(*args_b, k)
    stage("up_a")
    whole = dl[...].reshape(tokens, vocab)
    ua[...] = dot(whole, w[:, :fa], ((1,), (0,))).reshape(ua.shape)
    for k in far:
        far_off(*args_a, k)
    stage("up_c")
    uc[...] = dot(whole, w[:, fa:fac], ((1,), (0,))).astype(BF16).reshape(uc.shape)
    r1c = Exchange("R1C", nx, x, at_x, lambda c: uc.at[:, c], rc.at[x], rc.at[0:nx - 1]).start()
    stage("fresh1")

    stage("hg")
    flat = whole.T
    hg[:, :fa] = dot(flat, na[...].reshape(tokens, fa), ((1,), (0,))).astype(BF16)
    hg[:, fa:fac] = dot(flat, nc[...].reshape(tokens, fc), ((1,), (0,))).astype(BF16)
    hg[:, fac:] = dot(flat, nbn[...].reshape(tokens, fb), ((1,), (0,))).astype(BF16)

    def summed(mine, arrived, me, n, index):
        acc = mine.astype(F32)
        for k in range(1, n):
            acc = acc + arrived[(lax.rem(me + k, n),) + index].astype(F32)
        return acc

    q2 = Exchange("QY", ny, y, at_y, lambda c: qy.at[y], qy.at[y], qy.at[0:ny - 1])
    q3 = Exchange("QZ", nz, z, at_z, lambda c: qz.at[z], qz.at[z], qz.at[0:nz - 1])
    r2a = copy("R2A", ra2.at[0:nx - 1], ra2.at[0:nx - 1], at_x(along[1]))
    r2b = copy("R2B", rb2.at[0:nx - 1], rb2.at[0:nx - 1], at_x(along[1]))
    r2c = Exchange("R2C", ny, y, at_y, lambda c: sc2.at[c], rc2.at[y], rc2.at[0:ny - 1])
    sends.extend([r2a, r2b])

    def turn_q2():
        q1.arrived()
        qy[y] = functools.reduce(jnp.add, [qx[s] for s in range(nx)])
        q2.start()

    def turn_q3():
        q2.arrived()
        qz[z] = functools.reduce(jnp.add, [qy[s] for s in range(ny)])
        q3.start()

    def turn_rc():
        r1c.arrived()
        for s in range(ny):
            sc2[s] = summed(uc[s, x], rc, x, nx, (s,)).astype(BF16)
        r2c.start()

    def row_b(k):
        sb2[k] = ended(back_b, own_b, rb, k).astype(BF16)
        if k:
            copy("R2B", sb2.at[k], rb2.at[x], at_x(along[k])).start()

    def row_a(k):
        sa2[k] = ended(back_a, own_a, ra, k).astype(BF16)
        if k:
            copy("R2A", sa2.at[k], ra2.at[x], at_x(along[k])).start()

    events = [(4.5, "turn_q2", turn_q2), (9.1, "turn_q3", turn_q3), (7.5, "turn_rc", turn_rc)]
    for i, k in enumerate(far):
        when = 3.5 + 0.7 * i
        events.append((when, f"rb{k}", functools.partial(two_off, *args_b, k)))
        events.append((when + 0.01, f"ra{k}", functools.partial(two_off, *args_a, k)))
        events.append((when + 0.02, f"nb{k}", functools.partial(next_to, *args_b, k)))
        events.append((when + 0.03, f"na{k}", functools.partial(next_to, *args_a, k)))
        when = 9.5 + 0.7 * i
        events.append((when, f"rowb{k}", functools.partial(row_b, k)))
        events.append((when + 0.01, f"rowa{k}", functools.partial(row_a, k)))
    for when, name, event in sorted(events, key=lambda e: e[0]):
        stage(name)
        event()

    stage("r2b_wait")
    r2b.wait_recv()
    stage("sum2b")
    asy[...] = summed(sb2[0], rb2, x, nx, ())
    for s in range(ny):
        s3y[s] = asy[s * rows:(s + 1) * rows, :]
    r4 = Exchange("R3Y", ny, y, at_y, lambda c: s3y.at[c], r3y.at[y], r3y.at[0:ny - 1]).start()
    stage("r2c_wait")
    r2c.arrived()
    asz[:, fa:] = summed(sc2[y], rc2, y, ny, ())
    stage("r2a_wait")
    r2a.wait_recv()
    stage("sum2")
    asz[:, :fa] = summed(sa2[0], ra2, x, nx, ())
    for s in range(nz):
        s3z[s] = asz[s * rows:(s + 1) * rows, :]
    r3 = Exchange("R3Z", nz, z, at_z, lambda c: s3z.at[c], r3z.at[z], r3z.at[0:nz - 1]).start()

    q3.arrived()
    stage("loss")
    losses = functools.reduce(jnp.add, [qz[s] for s in range(nz)]) + logs[0]
    spot = lax.broadcasted_iota(jnp.int32, (1, tokens), 1)
    for i in range(rows):
        loss[:, i:i + 1] = jnp.sum(jnp.where(spot == f * rows + i, losses, 0.0), axis=-1, keepdims=True)

    stage("r3_wait")
    r3.arrived()
    r4.arrived()
    stage("final")
    upstream = jnp.concatenate([summed(s3z[z], r3z, z, nz, ()), summed(s3y[y], r3y, y, ny, ())], axis=-1)
    scaled = gain[...] * upstream
    inner = jnp.mean(scaled * values, axis=-1, keepdims=True)
    hd[...] = (inverse * scaled - values * (inverse * inverse * inverse) * inner).astype(BF16)

    stage("sent_wait")
    for all_sent in sends:
        all_sent.wait_send()
    other.wait_send()
    stage(None)


def finish_kernel(*refs):
    half = len(refs) // 2
    copies = [pltpu.make_async_copy(a, b, refs[-1].at[i]) for i, (a, b) in enumerate(zip(refs[:half], refs[half:-1]))]
    for copy in copies:
        copy.start()
    for copy in copies:
        copy.wait()


def finish(*arrays):
    n = len(arrays)
    return pl.pallas_call(
        finish_kernel,
        out_shape=tuple(jax.ShapeDtypeStruct(a.shape, a.dtype) for a in arrays),
        in_specs=[pl.BlockSpec(memory_space=pltpu.VMEM)] * n,
        out_specs=[pl.BlockSpec(memory_space=pl.ANY)] * n,
        scratch_shapes=[pltpu.SemaphoreType.DMA((n,))],
        compiler_params=pltpu.CompilerParams(vmem_limit_bytes=2**20),
        name="finish",
    )(*arrays)


def body(hidden, gain, head, labels):
    rows, feat = hidden.shape[1:]
    vocab = head.shape[2]
    tokens = labels.shape[0]
    ny, nx, nz = dims = GRID[tokens // rows]
    fa, fc, fb = parts = SPLIT[feat]
    fac = fa + fc
    gz, gy = nz * rows, ny * rows
    vm = pltpu.VMEM
    loss, head_grad, hidden_grad = pl.pallas_call(
        functools.partial(kernel, dims, parts),
        out_shape=(
            vm((1, rows), F32),
            vm((vocab, feat), BF16),
            vm((rows, feat), BF16),
        ),
        in_specs=[pl.BlockSpec(memory_space=pltpu.HBM)] * 4,
        out_specs=[pl.BlockSpec(memory_space=vm)] * 3,
        scratch_shapes=[
            vm((vocab, feat), BF16),
            vm((rows, feat), BF16),
            vm((nz, rows, fac), BF16),
            vm((ny, rows, fb), BF16),
            vm((gz, fac), F32),
            vm((gy, fb), F32),
            vm((ny, nx, gz, fa), BF16),
            vm((ny, nx, gz, fc), BF16),
            vm((nx, nz, gy, fb), BF16),
            vm((ny, nx, gz, fb), BF16),
            vm((tokens, vocab), F32),
            vm((tokens, vocab), F32),
            vm((nz, 2, tokens), F32),
            vm((ny, 2, tokens), F32),
            vm((2 * nx, 2, tokens), F32),
            vm((tokens, 128), F32),
            vm((tokens, 128), jnp.int32),
            vm((ny, nx, gz, vocab), BF16),
            vm((nx, nz, gy, vocab), BF16),
            vm((ny, nx, gz, fa), F32),
            vm((ny, nx, gz, fc), BF16),
            vm((nx, nz, gy, fb), F32),
            vm((ny * nx, gz, fa), BF16),
            vm((nz * nx, gy, fb), BF16),
            vm((ny * nx, gz, fa), BF16),
            vm((nx, ny, gz, fc), BF16),
            vm((nz * nx, gy, fb), BF16),
            vm((nx, gz, fa), BF16),
            vm((ny, gz, fc), BF16),
            vm((nx, gy, fb), BF16),
            vm((nx, gz, fa), BF16),
            vm((ny, gz, fc), BF16),
            vm((nx, gy, fb), BF16),
            vm((nz, rows, fac), F32),
            vm((ny, rows, fb), F32),
            vm((nz, rows, fac), F32),
            vm((ny, rows, fb), F32),
            vm((nz, 1, tokens), F32),
            vm((ny, 1, tokens), F32),
            vm((nx, 1, tokens), F32),
            pltpu.SemaphoreType.DMA((len(NUM),)),
            pltpu.SemaphoreType.DMA((len(NUM),)),
            pltpu.SemaphoreType.DMA((len(RINGS), max(ny, nz) * nx)),
            pltpu.SemaphoreType.DMA((2, nx)),
            pltpu.SemaphoreType.DMA((4,)),
            vm((rows, feat), BF16),
            vm((1, feat), F32),
            vm((1, tokens), jnp.int32),
        ],
        compiler_params=pltpu.CompilerParams(collective_id=0, has_side_effects=True, vmem_limit_bytes=123 * 2**19),
        name="head_step",
    )(hidden[0], gain, head[0].T, labels.reshape(1, tokens))
    loss, head_grad, hidden_grad = finish(loss, head_grad, hidden_grad)
    return loss, head_grad.T[None], hidden_grad[None]


def solution(mesh):
    in_specs = (P("member", "fsdp", None), P("member", None), P("member", None, "fsdp"), P())
    out_specs = (P("member", "fsdp"), P("member", None, "fsdp"), P("member", "fsdp", None))
    return jax.shard_map(body, mesh=mesh, in_specs=in_specs, out_specs=out_specs, check_vma=False)
```

```python
import functools
import math

import jax
import jax.numpy as jnp
from jax import lax
from jax.experimental import pallas as pl
from jax.experimental.pallas import tpu as pltpu
from jax.sharding import PartitionSpec as P

EPS = 1e-05
BETA = 0.5
MESH = pl.DeviceIdType.MESH
F32 = jnp.float32
BF16 = jnp.bfloat16
GRID = {256: (8, 4, 8), 8: (2, 2, 2), 16: (4, 2, 2), 32: (8, 2, 2)}
SPLIT = {2048: (640, 512, 896), 384: (128, 128, 128)}

NAMES = [
    "G1Z", "G1Y", "G2A", "G2B", "G2C", "G3C", "SZ", "SY", "SX", "TE", "R1C", "R2A", "R2B", "R2C", "R3Z", "R3Y",
    "QX", "QY", "QZ", "GA", "GB", "RA", "RB",
]
NUM = {name: i for i, name in enumerate(NAMES)}
RINGS = {"GA": 0, "GB": 1, "RA": 0, "RB": 1}
TRACE = False


def dot(a, b, dims):
    return lax.dot_general(a, b, (dims, ((), ())), preferred_element_type=F32)


def kernel(
    dims, parts, hid_in, gain_in, head_hbm, lab_in, loss, hg, hd,
    w, own, z1, y1, asz, asy, na, nc, nb, nbn, lg, tch, stz, sty, stx, ltt, labt,
    dl, dlb, ua, uc, ub, pa, pb, ra, rc, rb, sa2, sc2, sb2, ra2, rc2, rb2,
    s3z, s3y, r3z, r3y, qz, qy, qx, ssem, rsem, gsem, xsem, csem, hid, gain, lab,
):
    ny, nx, nz = dims
    fa, fc, fb = parts
    fac = fa + fc
    rows, feat = hid.shape
    tokens = lab.shape[1]
    vocab = head_hbm.shape[0]
    gz, gy = nz * rows, ny * rows

    f = lax.axis_index("fsdp")
    mem = lax.axis_index("member")
    z = lax.rem(f, nz)
    x = lax.rem(lax.div(f, nz), nx)
    y = lax.div(f, nz * nx)

    def at_z(c):
        return {"fsdp": f - z + c}

    def at_x(c):
        return {"fsdp": f + (c - x) * nz}

    def at_y(c):
        return {"fsdp": f + (c - y) * (nx * nz)}

    def copy(name, src, dst, dev, slot=None, sems=None):
        num = NUM[name]
        arrive = rsem.at[num] if slot is None else (gsem.at[RINGS[name], slot] if sems is None else sems.at[slot])
        return pltpu.make_async_remote_copy(
            src_ref=src, dst_ref=dst, send_sem=ssem.at[num], recv_sem=arrive, device_id=dev, device_id_type=MESH
        )

    sends = []
    near = sorted(range(nx), key=lambda k: min(k, nx - k))
    upward = near[0::2]
    along = [lax.rem(x + k, nx) for k in range(nx)]

    class Exchange:
        def __init__(self, name, n, me, at, src, dst, many):
            self.n, self.me, self.at = n, me, at
            self.make = lambda c: copy(name, src(c), dst, at(c))
            self.all = copy(name, many, many, at(lax.rem(me + 1, n)))
            sends.append(self.all)

        def start(self):
            def step(k, carry):
                self.make(lax.rem(self.me + k, self.n)).start()
                return carry

            lax.fori_loop(1, self.n, step, 0)
            return self

        def arrived(self):
            self.all.wait_recv()

    class Ring:
        def __init__(self, name, n, me, at, many):
            self.name, self.n, self.me, self.at = name, n, me, at
            self.half = n // 2
            self.pending = set()
            sends.append(copy(name, many, many, at(lax.rem(me + 1, n))))

        def other(self, way, steps):
            return lax.rem(self.me + (steps if way == 0 else self.n - steps), self.n)

        def reaches(self, way, d, k):
            return d < self.half or (d == self.half and (k in upward) == (way == 0))

        def slot(self, way, d, k):
            return (way * self.half + d - 1) * nx + k

        def send(self, way, d, k, hops, src, dst):
            copy(self.name, src, dst, self.at(self.other(way, hops)), self.slot(way, d, k)).start()
            self.pending.add((way, d, k))

        def arrived(self, way, d, k, ref):
            self.pending.remove((way, d, k))
            copy(self.name, ref, ref, self.at(self.other(way, 1)), self.slot(way, d, k)).wait_recv()

    scope = []

    def stage(name):
        if TRACE:
            if scope:
                scope.pop().__exit__(None, None, None)
            if name:
                scope.append(jax.named_scope(name))
                scope[0].__enter__()

    stage("greet")
    loads = [
        pltpu.make_async_copy(src, dst, csem.at[i])
        for i, (src, dst) in enumerate([(hid_in, hid), (gain_in, gain), (lab_in, lab), (head_hbm, w)])
    ]
    for load in loads:
        load.start()

    barrier = pltpu.get_barrier_semaphore()

    def greet(dev):
        pl.semaphore_signal(barrier, inc=1, device_id=dev, device_id_type=MESH)

    def greet_all(n, me, at):
        def step(k, carry):
            greet(at(lax.rem(me + k, n)))
            return carry

        lax.fori_loop(1, n, step, 0)

    greet_all(nz, z, at_z)
    greet_all(ny, y, at_y)
    greet_all(nx, x, at_x)
    def at_x_other(c):
        return {"member": 1 - mem, "fsdp": f + (c - x) * nz}

    def greet_other(c, carry):
        greet(at_x_other(c))
        return carry

    lax.fori_loop(0, nx, greet_other, 0)

    loads[0].wait()
    loads[1].wait()
    values = hid[...].astype(F32)
    inverse = lax.rsqrt(jnp.mean(values * values, axis=-1, keepdims=True) + EPS)
    own[...] = (values * inverse * gain[...]).astype(BF16)

    stage("barrier")
    pl.semaphore_wait(barrier, nz - 1 + ny - 1 + nx - 1 + nx)

    stage("g1start")
    g1y = Exchange("G1Y", ny, y, at_y, lambda c: own.at[:, pl.ds(fac, fb)], y1.at[y], y1.at[0:ny - 1]).start()
    g1z = Exchange("G1Z", nz, z, at_z, lambda c: own.at[:, pl.ds(0, fac)], z1.at[z], z1.at[0:nz - 1]).start()

    z1[z] = own[:, :fac]
    y1[y] = own[:, fac:]
    loads[2].wait()
    labt[...] = jnp.broadcast_to(lab[...], (128, tokens)).T.reshape(labt.shape)
    size = ny * gz
    lr = int(math.log2(rows))
    lz = int(math.log2(nz))
    to = lax.broadcasted_iota(jnp.int32, (size, size), 0)
    frm = lax.broadcasted_iota(jnp.int32, (size, size), 1)
    ty = to >> (lr + lz)
    tz = (to >> lr) & (nz - 1)
    perm = (frm == tz * gy + ty * rows + (to & (rows - 1))).astype(BF16)

    stage("g1y_wait")
    g1y.arrived()
    for s in range(ny):
        asy[s * rows:(s + 1) * rows, :] = y1[s].astype(F32)
    nb[x, z] = asy[...].astype(BF16)

    def to_row(name, which, ref):
        for k in near[1:]:
            copy(name, ref, ref, at_x(along[k]), nx - k, xsem.at[which]).start()

    def from_row(name, which, ref, k):
        copy(name, ref, ref, at_x(along[k]), k, xsem.at[which]).wait_recv()

    def block_a(b, k):
        return na.at[b, along[k]]

    def block_b(b, k):
        return nb.at[along[k], b]

    sends.append(copy("G2A", na.at[0, 0:nx - 1], na.at[0, 0:nx - 1], at_x(along[1])))
    sends.append(copy("G2B", nb.at[0:nx - 1, 0], nb.at[0:nx - 1, 0], at_x(along[1])))
    ring_a = Ring("GA", ny, y, at_y, na.at[0:ny - 1])
    ring_b = Ring("GB", nz, z, at_z, nb.at[:, 0:nz - 1])

    def hand_on(ring, block, late, k, hops=(2, 1)):
        back = 2 * late
        for way in range(2):
            if late:
                if not ring.reaches(way, 3, k):
                    continue
                ring.arrived(way, 2, k, block(ring.other(1 - way, 2), k))
            ref = block(ring.other(1 - way, back) if back else ring.me, k)
            for hop in hops:
                if ring.reaches(way, back + hop, k):
                    ring.send(way, back + hop, k, hop, ref, ref)

    def rest(ring, block, k):
        for way, d, _ in sorted(p for p in ring.pending if p[2] == k):
            ring.arrived(way, d, k, block(ring.other(1 - way, d), k))

    to_row("G2B", 1, nb.at[x, z])
    hand_on(ring_b, block_b, 0, 0)
    stage("g1z_wait")
    g1z.arrived()
    for s in range(nz):
        asz[s * rows:(s + 1) * rows, :] = z1[s].astype(F32)
    tile = asz[...].astype(BF16)
    na[y, x] = tile[:, :fa]
    to_row("G2A", 0, na.at[y, x])
    nc[y, x] = tile[:, fa:]
    g2c = Exchange("G2C", ny, y, at_y, lambda c: nc.at[y, x], nc.at[y, x], nc.at[0:ny - 1, 0]).start()
    hand_on(ring_a, block_a, 0, 0)

    def step_b(s, k):
        if s == 0:
            from_row("G2B", 1, nb.at[along[k], z], k)
        hand_on(ring_b, block_b, s, k, (2, 1) if s else (2,))

    def step_a(s, k):
        if s == 0:
            from_row("G2A", 0, na.at[y, along[k]], k)
        hand_on(ring_a, block_a, s, k, (2, 1) if s else (2,))

    def step_1(k):
        hand_on(ring_b, block_b, 0, k, (1,))
        hand_on(ring_a, block_a, 0, k, (1,))

    g3c = Exchange("G3C", nx, x, at_x, lambda c: nc.at[:, x], nc.at[:, x], nc.at[:, 0:nx - 1])

    def turn_c():
        g2c.arrived()
        g3c.start()

    events = [(4.0, "turn_c", turn_c)]
    for k in near[1:]:
        events.append((3.3 + 0.01 * k, f"n{k}", functools.partial(step_1, k)))
    for s in range(2):
        for k in range(nx):
            if (s, k) == (0, 0):
                continue
            when = 3.5 * s + 1.5 * min(k, nx - k) + 0.1 * k
            events.append((when, f"b{s}{k}", functools.partial(step_b, s, k)))
            events.append((when + 0.01, f"a{s}{k}", functools.partial(step_a, s, k)))
    for when, name, event in sorted(events, key=lambda e: e[0]):
        stage(name)
        event()

    stage("load_wait")
    loads[3].wait()
    stage("g3c_wait")
    g3c.arrived()

    def joined(parts):
        return jnp.concatenate([p.reshape(size, p.shape[-1]) for p in parts], axis=0)

    def lanes(k):
        return pl.ds(pl.multiple_of(along[k] * size, size), size)

    for group in (near[:nx // 2], near[nx // 2:]):
        for k in group:
            stage(f"rest{k}")
            rest(ring_b, block_b, k)
            rest(ring_a, block_a, k)
        stage(f"logits{group[0]}")
        for k in group:
            swap = dot(perm, nb[along[k]].reshape(size, fb), ((1,), (0,)))
            nbn[:, along[k]] = swap.astype(BF16).reshape(ny, gz, fb)
        logits = (
            dot(joined([nc[:, along[k]] for k in group]), w[:, fa:fac], ((1,), (1,)))
            + dot(joined([na[:, along[k]] for k in group]), w[:, :fa], ((1,), (1,)))
            + dot(joined([nbn[:, along[k]] for k in group]), w[:, fac:], ((1,), (1,)))
        )
        top = jnp.max(logits, axis=-1, keepdims=True)
        total = jnp.sum(jnp.exp(logits - top), axis=-1, keepdims=True)
        lane = lax.broadcasted_iota(jnp.int32, (logits.shape[0], 128), 1)
        both = jnp.where(lane == 0, top, total).T
        for i, k in enumerate(group):
            lg[along[k]] = logits[i * size:(i + 1) * size, :]
            stz[z, :, lanes(k)] = both[0:2, i * size:(i + 1) * size]

    def merged(blocks):
        best = functools.reduce(jnp.maximum, [b[0:1, :] for b in blocks])
        return best, functools.reduce(jnp.add, [b[1:2, :] * jnp.exp(b[0:1, :] - best) for b in blocks])

    sz = Exchange("SZ", nz, z, at_z, lambda c: stz.at[z], stz.at[z], stz.at[0:nz - 1]).start()
    stage("sz_wait")
    other = copy("TE", lg, tch, {"member": 1 - mem})
    other.start()
    sz.arrived()
    stage("mergez")
    best, total = merged([stz[s] for s in range(nz)])
    sty[y, 0:1, :] = best
    sty[y, 1:2, :] = total
    sy = Exchange("SY", ny, y, at_y, lambda c: sty.at[y], sty.at[y], sty.at[0:ny - 1]).start()
    stage("sy_wait")
    sy.arrived()
    stage("mergey")
    best, total = merged([sty[s] for s in range(ny)])
    mine = mem * nx + x
    stx[mine, 0:1, :] = best
    stx[mine, 1:2, :] = total

    sx = Exchange("SX", nx, x, at_x, lambda c: stx.at[mine], stx.at[mine], stx.at[0:2 * nx - 1]).start()

    def cross_step(k, carry):
        copy("SX", stx.at[mine], stx.at[mine], at_x_other(lax.rem(x + k, nx))).start()
        return carry

    lax.fori_loop(0, nx, cross_step, 0)
    stage("sx_wait")
    sx.arrived()
    stage("mergex")
    logs = []
    for who in (mem, 1 - mem):
        best, total = merged([stx[who * nx + s] for s in range(nx)])
        logs.append(best + jnp.log(total))
    row = lax.broadcasted_iota(jnp.int32, (128, tokens), 0)
    ltt[...] = jnp.where(row == 0, logs[0], logs[1]).T.reshape(ltt.shape)

    stage("teacher_wait")
    other.wait_recv()
    stage("dlogits")
    columns = lax.broadcasted_iota(jnp.int32, (size, vocab), 1)

    def logits_back(k):
        local = labt[:, along[k]].reshape(size, 128)[:, 0:1] - f * vocab
        mask = local == columns
        logits = lg[along[k]]
        log_total = ltt[along[k]][:, 0:1]
        target = jnp.exp((tch[along[k]] - ltt[along[k]][:, 1:2]).astype(BF16).astype(F32))
        student = jnp.exp(logits - log_total)
        grad = ((1.0 + BETA) * student - mask.astype(F32) - BETA * target) * (1.0 / tokens)
        grad = grad.astype(BF16)
        dl[:, along[k]] = grad.reshape(ny, gz, vocab)
        dlb[along[k]] = dot(perm, grad, ((0,), (0,))).astype(BF16).reshape(nz, gy, vocab)
        part = jnp.sum(
            BETA * target * (log_total - logits) - jnp.where(mask, logits, 0.0), axis=-1, keepdims=True
        )
        qx[x, :, lanes(k)] = jnp.broadcast_to(part, (size, 128)).T[0:1, :]

    back_b = Ring("RB", nz, z, at_z, pb.at[0:(nz - 1) * nx])
    back_a = Ring("RA", ny, y, at_y, pa.at[0:(ny - 1) * nx])

    def own_a(b, k):
        return ua[b, along[k]]

    def own_b(b, k):
        return ub[along[k], b]

    def send_on(ring, put, got, way, d, k, hops, acc):
        here = ring.slot(way, d, k)
        put[here] = acc.astype(BF16)
        ring.send(way, d, k, hops, put.at[here], got.at[here])

    def taken(ring, got, way, d, k, acc):
        if (way, d, k) in ring.pending:
            here = ring.slot(way, d, k)
            ring.arrived(way, d, k, got.at[here])
            acc = acc + got[here].astype(F32)
        return acc

    def far_off(ring, own_of, put, got, k):
        for d in (4, 3):
            for way in range(2):
                if ring.reaches(way, d, k):
                    send_on(ring, put, got, way, d, k, d - 2, own_of(ring.other(way, d), k))

    def next_to(ring, own_of, put, got, k):
        for way in range(2):
            if ring.reaches(way, 1, k):
                send_on(ring, put, got, way, 1, k, 1, own_of(ring.other(way, 1), k))

    def two_off(ring, own_of, put, got, k):
        for way in range(2):
            if ring.reaches(way, 2, k):
                acc = own_of(ring.other(way, 2), k)
                for d in (3, 4):
                    acc = taken(ring, got, way, d, k, acc)
                send_on(ring, put, got, way, 2, k, 2, acc)

    def ended(ring, own_of, got, k):
        acc = own_of(ring.me, k)
        for d in (1, 2):
            for way in range(2):
                acc = taken(ring, got, way, d, k, acc)
        return acc

    far = near[::-1]
    args_a = back_a, own_a, pa, ra
    args_b = back_b, own_b, pb, rb

    for group in (far[:nx // 2], far[nx // 2:]):
        stage(f"dlogits{group[0]}")
        for k in group:
            logits_back(k)
        stage(f"up_b{group[0]}")
        rise = dot(joined([dlb[along[k]] for k in group]), w[:, fac:], ((1,), (0,)))
        for i, k in enumerate(group):
            ub[along[k]] = rise[i * size:(i + 1) * size, :].reshape(nz, gy, fb)
            far_off(*args_b, k)
        stage(f"up_a{group[0]}")
        rise = dot(joined([dl[:, along[k]] for k in group]), w[:, :fa], ((1,), (0,)))
        for i, k in enumerate(group):
            ua[:, along[k]] = rise[i * size:(i + 1) * size, :].reshape(ny, gz, fa)
            far_off(*args_a, k)
    stage("up_c")
    q1 = Exchange("QX", nx, x, at_x, lambda c: qx.at[x], qx.at[x], qx.at[0:nx - 1]).start()
    whole = dl[...].reshape(tokens, vocab)
    uc[...] = dot(whole, w[:, fa:fac], ((1,), (0,))).astype(BF16).reshape(uc.shape)
    r1c = Exchange("R1C", nx, x, at_x, lambda c: uc.at[:, c], rc.at[x], rc.at[0:nx - 1]).start()
    stage("fresh1")

    stage("hg")
    flat = whole.T
    hg[:, :fa] = dot(flat, na[...].reshape(tokens, fa), ((1,), (0,))).astype(BF16)
    hg[:, fa:fac] = dot(flat, nc[...].reshape(tokens, fc), ((1,), (0,))).astype(BF16)
    hg[:, fac:] = dot(flat, nbn[...].reshape(tokens, fb), ((1,), (0,))).astype(BF16)

    def summed(mine, arrived, me, n, index):
        acc = mine.astype(F32)
        for k in range(1, n):
            acc = acc + arrived[(lax.rem(me + k, n),) + index].astype(F32)
        return acc

    q2 = Exchange("QY", ny, y, at_y, lambda c: qy.at[y], qy.at[y], qy.at[0:ny - 1])
    q3 = Exchange("QZ", nz, z, at_z, lambda c: qz.at[z], qz.at[z], qz.at[0:nz - 1])
    r2a = copy("R2A", ra2.at[0:nx - 1], ra2.at[0:nx - 1], at_x(along[1]))
    r2b = copy("R2B", rb2.at[0:nx - 1], rb2.at[0:nx - 1], at_x(along[1]))
    r2c = Exchange("R2C", ny, y, at_y, lambda c: sc2.at[c], rc2.at[y], rc2.at[0:ny - 1])
    sends.extend([r2a, r2b])

    def turn_q2():
        q1.arrived()
        qy[y] = functools.reduce(jnp.add, [qx[s] for s in range(nx)])
        q2.start()

    def turn_q3():
        q2.arrived()
        qz[z] = functools.reduce(jnp.add, [qy[s] for s in range(ny)])
        q3.start()

    def turn_rc():
        r1c.arrived()
        for s in range(ny):
            sc2[s] = summed(uc[s, x], rc, x, nx, (s,)).astype(BF16)
        r2c.start()

    def row_b(k):
        sb2[k] = ended(back_b, own_b, rb, k).astype(BF16)
        if k:
            copy("R2B", sb2.at[k], rb2.at[x], at_x(along[k])).start()

    def row_a(k):
        sa2[k] = ended(back_a, own_a, ra, k).astype(BF16)
        if k:
            copy("R2A", sa2.at[k], ra2.at[x], at_x(along[k])).start()

    events = [(4.5, "turn_q2", turn_q2), (9.1, "turn_q3", turn_q3), (7.5, "turn_rc", turn_rc)]
    for i, k in enumerate(far):
        when = 3.5 + 0.7 * i
        events.append((when, f"rb{k}", functools.partial(two_off, *args_b, k)))
        events.append((when + 0.01, f"ra{k}", functools.partial(two_off, *args_a, k)))
        events.append((when + 0.02, f"nb{k}", functools.partial(next_to, *args_b, k)))
        events.append((when + 0.03, f"na{k}", functools.partial(next_to, *args_a, k)))
        when = 9.5 + 0.7 * i
        events.append((when, f"rowb{k}", functools.partial(row_b, k)))
        events.append((when + 0.01, f"rowa{k}", functools.partial(row_a, k)))
    for when, name, event in sorted(events, key=lambda e: e[0]):
        stage(name)
        event()

    stage("r2b_wait")
    r2b.wait_recv()
    stage("sum2b")
    asy[...] = summed(sb2[0], rb2, x, nx, ())
    for s in range(ny):
        s3y[s] = asy[s * rows:(s + 1) * rows, :]
    r4 = Exchange("R3Y", ny, y, at_y, lambda c: s3y.at[c], r3y.at[y], r3y.at[0:ny - 1]).start()
    stage("r2c_wait")
    r2c.arrived()
    asz[:, fa:] = summed(sc2[y], rc2, y, ny, ())
    stage("r2a_wait")
    r2a.wait_recv()
    stage("sum2")
    asz[:, :fa] = summed(sa2[0], ra2, x, nx, ())
    for s in range(nz):
        s3z[s] = asz[s * rows:(s + 1) * rows, :]
    r3 = Exchange("R3Z", nz, z, at_z, lambda c: s3z.at[c], r3z.at[z], r3z.at[0:nz - 1]).start()

    q3.arrived()
    stage("loss")
    losses = functools.reduce(jnp.add, [qz[s] for s in range(nz)]) + logs[0]
    spot = lax.broadcasted_iota(jnp.int32, (1, tokens), 1)
    for i in range(rows):
        loss[:, i:i + 1] = jnp.sum(jnp.where(spot == x * size + y * gz + z * rows + i, losses, 0.0), axis=-1, keepdims=True)

    stage("r3_wait")
    r3.arrived()
    r4.arrived()
    stage("final")
    upstream = jnp.concatenate([summed(s3z[z], r3z, z, nz, ()), summed(s3y[y], r3y, y, ny, ())], axis=-1)
    scaled = gain[...] * upstream
    inner = jnp.mean(scaled * values, axis=-1, keepdims=True)
    hd[...] = (inverse * scaled - values * (inverse * inverse * inverse) * inner).astype(BF16)

    stage("sent_wait")
    for all_sent in sends:
        all_sent.wait_send()
    other.wait_send()
    stage(None)


def finish_kernel(*refs):
    half = len(refs) // 2
    copies = [pltpu.make_async_copy(a, b, refs[-1].at[i]) for i, (a, b) in enumerate(zip(refs[:half], refs[half:-1]))]
    for copy in copies:
        copy.start()
    for copy in copies:
        copy.wait()


def finish(*arrays):
    n = len(arrays)
    return pl.pallas_call(
        finish_kernel,
        out_shape=tuple(jax.ShapeDtypeStruct(a.shape, a.dtype) for a in arrays),
        in_specs=[pl.BlockSpec(memory_space=pltpu.VMEM)] * n,
        out_specs=[pl.BlockSpec(memory_space=pl.ANY)] * n,
        scratch_shapes=[pltpu.SemaphoreType.DMA((n,))],
        compiler_params=pltpu.CompilerParams(vmem_limit_bytes=2**20),
        name="finish",
    )(*arrays)


def body(hidden, gain, head, labels):
    rows, feat = hidden.shape[1:]
    vocab = head.shape[2]
    tokens = labels.shape[0]
    ny, nx, nz = dims = GRID[tokens // rows]
    fa, fc, fb = parts = SPLIT[feat]
    fac = fa + fc
    gz, gy = nz * rows, ny * rows
    vm = pltpu.VMEM
    loss, head_grad, hidden_grad = pl.pallas_call(
        functools.partial(kernel, dims, parts),
        out_shape=(
            vm((1, rows), F32),
            vm((vocab, feat), BF16),
            vm((rows, feat), BF16),
        ),
        in_specs=[pl.BlockSpec(memory_space=pltpu.HBM)] * 4,
        out_specs=[pl.BlockSpec(memory_space=vm)] * 3,
        scratch_shapes=[
            vm((vocab, feat), BF16),
            vm((rows, feat), BF16),
            vm((nz, rows, fac), BF16),
            vm((ny, rows, fb), BF16),
            vm((gz, fac), F32),
            vm((gy, fb), F32),
            vm((ny, nx, gz, fa), BF16),
            vm((ny, nx, gz, fc), BF16),
            vm((nx, nz, gy, fb), BF16),
            vm((ny, nx, gz, fb), BF16),
            vm((nx, ny * gz, vocab), F32),
            vm((nx, ny * gz, vocab), F32),
            vm((nz, 2, tokens), F32),
            vm((ny, 2, tokens), F32),
            vm((2 * nx, 2, tokens), F32),
            vm((nx, ny * gz, 128), F32),
            vm((ny, nx, gz, 128), jnp.int32),
            vm((ny, nx, gz, vocab), BF16),
            vm((nx, nz, gy, vocab), BF16),
            vm((ny, nx, gz, fa), F32),
            vm((ny, nx, gz, fc), BF16),
            vm((nx, nz, gy, fb), F32),
            vm((ny * nx, gz, fa), BF16),
            vm((nz * nx, gy, fb), BF16),
            vm((ny * nx, gz, fa), BF16),
            vm((nx, ny, gz, fc), BF16),
            vm((nz * nx, gy, fb), BF16),
            vm((nx, gz, fa), BF16),
            vm((ny, gz, fc), BF16),
            vm((nx, gy, fb), BF16),
            vm((nx, gz, fa), BF16),
            vm((ny, gz, fc), BF16),
            vm((nx, gy, fb), BF16),
            vm((nz, rows, fac), F32),
            vm((ny, rows, fb), F32),
            vm((nz, rows, fac), F32),
            vm((ny, rows, fb), F32),
            vm((nz, 1, tokens), F32),
            vm((ny, 1, tokens), F32),
            vm((nx, 1, tokens), F32),
            pltpu.SemaphoreType.DMA((len(NUM),)),
            pltpu.SemaphoreType.DMA((len(NUM),)),
            pltpu.SemaphoreType.DMA((2, max(ny, nz) * nx)),
            pltpu.SemaphoreType.DMA((2, nx)),
            pltpu.SemaphoreType.DMA((4,)),
            vm((rows, feat), BF16),
            vm((1, feat), F32),
            vm((1, tokens), jnp.int32),
        ],
        compiler_params=pltpu.CompilerParams(collective_id=0, has_side_effects=True, vmem_limit_bytes=123 * 2**19),
        name="head_step",
    )(hidden[0], gain, head[0].T, labels.reshape(1, tokens))
    loss, head_grad, hidden_grad = finish(loss, head_grad, hidden_grad)
    return loss, head_grad.T[None], hidden_grad[None]


def solution(mesh):
    in_specs = (P("member", "fsdp", None), P("member", None), P("member", None, "fsdp"), P())
    out_specs = (P("member", "fsdp"), P("member", None, "fsdp"), P("member", "fsdp", None))
    return jax.shard_map(body, mesh=mesh, in_specs=in_specs, out_specs=out_specs, check_vma=False)
```

```python
import functools
import math

import jax
import jax.numpy as jnp
from jax import lax
from jax.experimental import pallas as pl
from jax.experimental.pallas import tpu as pltpu
from jax.sharding import PartitionSpec as P

EPS = 1e-05
BETA = 0.5
MESH = pl.DeviceIdType.MESH
F32 = jnp.float32
BF16 = jnp.bfloat16
GRID = {256: (8, 4, 8), 8: (2, 2, 2), 16: (4, 2, 2), 32: (8, 2, 2)}
SPLIT = {2048: (640, 512, 896), 384: (128, 128, 128)}

NAMES = [
    "G1Z", "G1Y", "G2A", "G2B", "G2C", "G3C", "SZ", "SY", "SX", "TE", "R1C", "R2A", "R2B", "R2C", "R3Z", "R3Y",
    "QX", "QY", "QZ", "GA", "GB", "RA", "RB",
]
NUM = {name: i for i, name in enumerate(NAMES)}
RINGS = {"GA": 0, "GB": 1, "RA": 0, "RB": 1}
TRACE = False


def dot(a, b, dims):
    return lax.dot_general(a, b, (dims, ((), ())), preferred_element_type=F32)


def farthest(n, j):
    odd = lax.rem(j, 2)
    return n // 2 + lax.div(j + 1, 2) * (1 - 2 * odd)


def kernel(
    dims, parts, hid_in, gain_in, head_hbm, lab_in, loss, hg, hd,
    w, own, z1, y1, asz, asy, na, nc, nb, nbn, lg, tch, stz, sty, stx, ltt, labt,
    dl, dlb, ua, uc, ub, pa, pb, ra, rc, rb, sa2, sc2, sb2, ra2, rc2, rb2,
    s3z, s3y, r3z, r3y, qz, qy, qx, ssem, rsem, gsem, xsem, csem, hid, gain, lab,
):
    ny, nx, nz = dims
    fa, fc, fb = parts
    fac = fa + fc
    rows, feat = hid.shape
    tokens = lab.shape[1]
    vocab = head_hbm.shape[0]
    gz, gy = nz * rows, ny * rows

    f = lax.axis_index("fsdp")
    mem = lax.axis_index("member")
    z = lax.rem(f, nz)
    x = lax.rem(lax.div(f, nz), nx)
    y = lax.div(f, nz * nx)

    def at_z(c):
        return {"fsdp": f - z + c}

    def at_x(c):
        return {"fsdp": f + (c - x) * nz}

    def at_y(c):
        return {"fsdp": f + (c - y) * (nx * nz)}

    def copy(name, src, dst, dev, slot=None, sems=None):
        num = NUM[name]
        arrive = rsem.at[num] if slot is None else (gsem.at[RINGS[name], slot] if sems is None else sems.at[slot])
        return pltpu.make_async_remote_copy(
            src_ref=src, dst_ref=dst, send_sem=ssem.at[num], recv_sem=arrive, device_id=dev, device_id_type=MESH
        )

    sends = []
    near = sorted(range(nx), key=lambda k: min(k, nx - k))
    upward = near[0::2]
    along = [lax.rem(x + k, nx) for k in range(nx)]

    class Exchange:
        def __init__(self, name, n, me, at, src, dst, many):
            self.n, self.me, self.at = n, me, at
            self.make = lambda c: copy(name, src(c), dst, at(c))
            self.all = copy(name, many, many, at(lax.rem(me + 1, n)))
            sends.append(self.all)

        def start(self):
            def step(j, carry):
                self.make(lax.rem(self.me + farthest(self.n, j), self.n)).start()
                return carry

            lax.fori_loop(0, self.n - 1, step, 0)
            return self

        def arrived(self):
            self.all.wait_recv()

    class Ring:
        def __init__(self, name, n, me, at, many):
            self.name, self.n, self.me, self.at = name, n, me, at
            self.half = n // 2
            self.pending = set()
            sends.append(copy(name, many, many, at(lax.rem(me + 1, n))))

        def other(self, way, steps):
            return lax.rem(self.me + (steps if way == 0 else self.n - steps), self.n)

        def reaches(self, way, d, k):
            return d < self.half or (d == self.half and (k in upward) == (way == 0))

        def slot(self, way, d, k):
            return (way * self.half + d - 1) * nx + k

        def send(self, way, d, k, hops, src, dst):
            copy(self.name, src, dst, self.at(self.other(way, hops)), self.slot(way, d, k)).start()
            self.pending.add((way, d, k))

        def arrived(self, way, d, k, ref):
            self.pending.remove((way, d, k))
            copy(self.name, ref, ref, self.at(self.other(way, 1)), self.slot(way, d, k)).wait_recv()

    scope = []

    def stage(name):
        if TRACE:
            if scope:
                scope.pop().__exit__(None, None, None)
            if name:
                scope.append(jax.named_scope(name))
                scope[0].__enter__()

    stage("greet")
    loads = [
        pltpu.make_async_copy(src, dst, csem.at[i])
        for i, (src, dst) in enumerate([(hid_in, hid), (gain_in, gain), (lab_in, lab), (head_hbm, w)])
    ]
    for load in loads:
        load.start()

    barrier = pltpu.get_barrier_semaphore()

    def greet(dev):
        pl.semaphore_signal(barrier, inc=1, device_id=dev, device_id_type=MESH)

    def greet_all(n, me, at):
        def step(j, carry):
            greet(at(lax.rem(me + farthest(n, j), n)))
            return carry

        lax.fori_loop(0, n - 1, step, 0)

    greet_all(nz, z, at_z)
    greet_all(ny, y, at_y)
    greet_all(nx, x, at_x)
    def at_x_other(c):
        return {"member": 1 - mem, "fsdp": f + (c - x) * nz}

    def greet_other(c, carry):
        greet(at_x_other(c))
        return carry

    lax.fori_loop(0, nx, greet_other, 0)

    loads[0].wait()
    loads[1].wait()
    values = hid[...].astype(F32)
    inverse = lax.rsqrt(jnp.mean(values * values, axis=-1, keepdims=True) + EPS)
    own[...] = (values * inverse * gain[...]).astype(BF16)

    stage("barrier")
    pl.semaphore_wait(barrier, nz - 1 + ny - 1 + nx - 1 + nx)

    stage("g1start")
    g1y = Exchange("G1Y", ny, y, at_y, lambda c: own.at[:, pl.ds(fac, fb)], y1.at[y], y1.at[0:ny - 1]).start()
    g1z = Exchange("G1Z", nz, z, at_z, lambda c: own.at[:, pl.ds(0, fac)], z1.at[z], z1.at[0:nz - 1]).start()

    z1[z] = own[:, :fac]
    y1[y] = own[:, fac:]
    loads[2].wait()
    labt[...] = jnp.broadcast_to(lab[...], (128, tokens)).T.reshape(labt.shape)
    size = ny * gz
    lr = int(math.log2(rows))
    lz = int(math.log2(nz))
    to = lax.broadcasted_iota(jnp.int32, (size, size), 0)
    frm = lax.broadcasted_iota(jnp.int32, (size, size), 1)
    ty = to >> (lr + lz)
    tz = (to >> lr) & (nz - 1)
    perm = (frm == tz * gy + ty * rows + (to & (rows - 1))).astype(BF16)

    stage("g1y_wait")
    g1y.arrived()
    for s in range(ny):
        asy[s * rows:(s + 1) * rows, :] = y1[s].astype(F32)
    nb[x, z] = asy[...].astype(BF16)

    def to_row(name, which, ref):
        for k in near[1:]:
            copy(name, ref, ref, at_x(along[k]), nx - k, xsem.at[which]).start()

    def from_row(name, which, ref, k):
        copy(name, ref, ref, at_x(along[k]), k, xsem.at[which]).wait_recv()

    def block_a(b, k):
        return na.at[b, along[k]]

    def block_b(b, k):
        return nb.at[along[k], b]

    sends.append(copy("G2A", na.at[0, 0:nx - 1], na.at[0, 0:nx - 1], at_x(along[1])))
    sends.append(copy("G2B", nb.at[0:nx - 1, 0], nb.at[0:nx - 1, 0], at_x(along[1])))
    ring_a = Ring("GA", ny, y, at_y, na.at[0:ny - 1])
    ring_b = Ring("GB", nz, z, at_z, nb.at[:, 0:nz - 1])

    def hand_on(ring, block, late, k, hops=(2, 1)):
        back = 2 * late
        for way in range(2):
            if late:
                if not ring.reaches(way, 3, k):
                    continue
                ring.arrived(way, 2, k, block(ring.other(1 - way, 2), k))
            ref = block(ring.other(1 - way, back) if back else ring.me, k)
            for hop in hops:
                if ring.reaches(way, back + hop, k):
                    ring.send(way, back + hop, k, hop, ref, ref)

    def rest(ring, block, k):
        for way, d, _ in sorted(p for p in ring.pending if p[2] == k):
            ring.arrived(way, d, k, block(ring.other(1 - way, d), k))

    to_row("G2B", 1, nb.at[x, z])
    hand_on(ring_b, block_b, 0, 0)
    stage("g1z_wait")
    g1z.arrived()
    for s in range(nz):
        asz[s * rows:(s + 1) * rows, :] = z1[s].astype(F32)
    tile = asz[...].astype(BF16)
    na[y, x] = tile[:, :fa]
    to_row("G2A", 0, na.at[y, x])
    nc[y, x] = tile[:, fa:]
    g2c = Exchange("G2C", ny, y, at_y, lambda c: nc.at[y, x], nc.at[y, x], nc.at[0:ny - 1, 0]).start()
    hand_on(ring_a, block_a, 0, 0)

    def step_b(s, k):
        if s == 0:
            from_row("G2B", 1, nb.at[along[k], z], k)
        hand_on(ring_b, block_b, s, k, (2, 1) if s else (2,))

    def step_a(s, k):
        if s == 0:
            from_row("G2A", 0, na.at[y, along[k]], k)
        hand_on(ring_a, block_a, s, k, (2, 1) if s else (2,))

    def step_1(k):
        hand_on(ring_b, block_b, 0, k, (1,))
        hand_on(ring_a, block_a, 0, k, (1,))

    g3c = Exchange("G3C", nx, x, at_x, lambda c: nc.at[:, x], nc.at[:, x], nc.at[:, 0:nx - 1])

    def turn_c():
        g2c.arrived()
        g3c.start()

    events = [(4.0, "turn_c", turn_c)]
    for k in near[1:]:
        events.append((3.3 + 0.01 * k, f"n{k}", functools.partial(step_1, k)))
    for s in range(2):
        for k in range(nx):
            if (s, k) == (0, 0):
                continue
            when = 3.5 * s + 1.5 * min(k, nx - k) + 0.1 * k
            events.append((when, f"b{s}{k}", functools.partial(step_b, s, k)))
            events.append((when + 0.01, f"a{s}{k}", functools.partial(step_a, s, k)))
    for when, name, event in sorted(events, key=lambda e: e[0]):
        stage(name)
        event()

    stage("load_wait")
    loads[3].wait()
    stage("g3c_wait")
    g3c.arrived()

    def joined(parts):
        return jnp.concatenate([p.reshape(size, p.shape[-1]) for p in parts], axis=0)

    def lanes(k):
        return pl.ds(pl.multiple_of(along[k] * size, size), size)

    for group in (near[:nx // 2], near[nx // 2:]):
        for k in group:
            stage(f"rest{k}")
            rest(ring_b, block_b, k)
            rest(ring_a, block_a, k)
        stage(f"logits{group[0]}")
        for k in group:
            swap = dot(perm, nb[along[k]].reshape(size, fb), ((1,), (0,)))
            nbn[:, along[k]] = swap.astype(BF16).reshape(ny, gz, fb)
        logits = (
            dot(joined([nc[:, along[k]] for k in group]), w[:, fa:fac], ((1,), (1,)))
            + dot(joined([na[:, along[k]] for k in group]), w[:, :fa], ((1,), (1,)))
            + dot(joined([nbn[:, along[k]] for k in group]), w[:, fac:], ((1,), (1,)))
        )
        top = jnp.max(logits, axis=-1, keepdims=True)
        total = jnp.sum(jnp.exp(logits - top), axis=-1, keepdims=True)
        lane = lax.broadcasted_iota(jnp.int32, (logits.shape[0], 128), 1)
        both = jnp.where(lane == 0, top, total).T
        for i, k in enumerate(group):
            lg[along[k]] = logits[i * size:(i + 1) * size, :]
            stz[z, :, lanes(k)] = both[0:2, i * size:(i + 1) * size]

    def merged(blocks):
        best = functools.reduce(jnp.maximum, [b[0:1, :] for b in blocks])
        return best, functools.reduce(jnp.add, [b[1:2, :] * jnp.exp(b[0:1, :] - best) for b in blocks])

    sz = Exchange("SZ", nz, z, at_z, lambda c: stz.at[z], stz.at[z], stz.at[0:nz - 1]).start()
    stage("sz_wait")
    other = copy("TE", lg, tch, {"member": 1 - mem})
    other.start()
    sz.arrived()
    stage("mergez")
    best, total = merged([stz[s] for s in range(nz)])
    sty[y, 0:1, :] = best
    sty[y, 1:2, :] = total
    sy = Exchange("SY", ny, y, at_y, lambda c: sty.at[y], sty.at[y], sty.at[0:ny - 1]).start()
    stage("sy_wait")
    sy.arrived()
    stage("mergey")
    best, total = merged([sty[s] for s in range(ny)])
    mine = mem * nx + x
    stx[mine, 0:1, :] = best
    stx[mine, 1:2, :] = total

    sx = Exchange("SX", nx, x, at_x, lambda c: stx.at[mine], stx.at[mine], stx.at[0:2 * nx - 1]).start()

    def cross_step(k, carry):
        copy("SX", stx.at[mine], stx.at[mine], at_x_other(lax.rem(x + k, nx))).start()
        return carry

    lax.fori_loop(0, nx, cross_step, 0)
    stage("sx_wait")
    sx.arrived()
    stage("mergex")
    logs = []
    for who in (mem, 1 - mem):
        best, total = merged([stx[who * nx + s] for s in range(nx)])
        logs.append(best + jnp.log(total))
    row = lax.broadcasted_iota(jnp.int32, (128, tokens), 0)
    ltt[...] = jnp.where(row == 0, logs[0], logs[1]).T.reshape(ltt.shape)

    stage("teacher_wait")
    other.wait_recv()
    stage("dlogits")
    columns = lax.broadcasted_iota(jnp.int32, (size, vocab), 1)

    def logits_back(k):
        local = labt[:, along[k]].reshape(size, 128)[:, 0:1] - f * vocab
        mask = local == columns
        logits = lg[along[k]]
        log_total = ltt[along[k]][:, 0:1]
        target = jnp.exp((tch[along[k]] - ltt[along[k]][:, 1:2]).astype(BF16).astype(F32))
        student = jnp.exp(logits - log_total)
        grad = ((1.0 + BETA) * student - mask.astype(F32) - BETA * target) * (1.0 / tokens)
        grad = grad.astype(BF16)
        dl[:, along[k]] = grad.reshape(ny, gz, vocab)
        dlb[along[k]] = dot(perm, grad, ((0,), (0,))).astype(BF16).reshape(nz, gy, vocab)
        part = jnp.sum(
            BETA * target * (log_total - logits) - jnp.where(mask, logits, 0.0), axis=-1, keepdims=True
        )
        qx[x, :, lanes(k)] = jnp.broadcast_to(part, (size, 128)).T[0:1, :]

    back_b = Ring("RB", nz, z, at_z, pb.at[0:(nz - 1) * nx])
    back_a = Ring("RA", ny, y, at_y, pa.at[0:(ny - 1) * nx])

    def own_a(b, k):
        return ua[b, along[k]]

    def own_b(b, k):
        return ub[along[k], b]

    def send_on(ring, put, got, way, d, k, hops, acc):
        here = ring.slot(way, d, k)
        put[here] = acc.astype(BF16)
        ring.send(way, d, k, hops, put.at[here], got.at[here])

    def taken(ring, got, way, d, k, acc):
        if (way, d, k) in ring.pending:
            here = ring.slot(way, d, k)
            ring.arrived(way, d, k, got.at[here])
            acc = acc + got[here].astype(F32)
        return acc

    def far_off(ring, own_of, put, got, k):
        for d in (4, 3):
            for way in range(2):
                if ring.reaches(way, d, k):
                    send_on(ring, put, got, way, d, k, d - 2, own_of(ring.other(way, d), k))

    def next_to(ring, own_of, put, got, k):
        for way in range(2):
            if ring.reaches(way, 1, k):
                send_on(ring, put, got, way, 1, k, 1, own_of(ring.other(way, 1), k))

    def two_off(ring, own_of, put, got, k):
        for way in range(2):
            if ring.reaches(way, 2, k):
                acc = own_of(ring.other(way, 2), k)
                for d in (3, 4):
                    acc = taken(ring, got, way, d, k, acc)
                send_on(ring, put, got, way, 2, k, 2, acc)

    def ended(ring, own_of, got, k):
        acc = own_of(ring.me, k)
        for d in (1, 2):
            for way in range(2):
                acc = taken(ring, got, way, d, k, acc)
        return acc

    far = near[::-1]
    args_a = back_a, own_a, pa, ra
    args_b = back_b, own_b, pb, rb

    for group in (far[:nx // 2], far[nx // 2:]):
        stage(f"dlogits{group[0]}")
        for k in group:
            logits_back(k)
        stage(f"up_b{group[0]}")
        rise = dot(joined([dlb[along[k]] for k in group]), w[:, fac:], ((1,), (0,)))
        for i, k in enumerate(group):
            ub[along[k]] = rise[i * size:(i + 1) * size, :].reshape(nz, gy, fb)
            far_off(*args_b, k)
        stage(f"up_a{group[0]}")
        rise = dot(joined([dl[:, along[k]] for k in group]), w[:, :fa], ((1,), (0,)))
        for i, k in enumerate(group):
            ua[:, along[k]] = rise[i * size:(i + 1) * size, :].reshape(ny, gz, fa)
            far_off(*args_a, k)
    stage("up_c")
    q1 = Exchange("QX", nx, x, at_x, lambda c: qx.at[x], qx.at[x], qx.at[0:nx - 1]).start()
    whole = dl[...].reshape(tokens, vocab)
    uc[...] = dot(whole, w[:, fa:fac], ((1,), (0,))).astype(BF16).reshape(uc.shape)
    r1c = Exchange("R1C", nx, x, at_x, lambda c: uc.at[:, c], rc.at[x], rc.at[0:nx - 1]).start()
    stage("fresh1")

    stage("hg")
    flat = whole.T
    hg[:, :fa] = dot(flat, na[...].reshape(tokens, fa), ((1,), (0,))).astype(BF16)
    hg[:, fa:fac] = dot(flat, nc[...].reshape(tokens, fc), ((1,), (0,))).astype(BF16)
    hg[:, fac:] = dot(flat, nbn[...].reshape(tokens, fb), ((1,), (0,))).astype(BF16)

    def summed(mine, arrived, me, n, index):
        acc = mine.astype(F32)
        for k in range(1, n):
            acc = acc + arrived[(lax.rem(me + k, n),) + index].astype(F32)
        return acc

    q2 = Exchange("QY", ny, y, at_y, lambda c: qy.at[y], qy.at[y], qy.at[0:ny - 1])
    q3 = Exchange("QZ", nz, z, at_z, lambda c: qz.at[z], qz.at[z], qz.at[0:nz - 1])
    r2a = copy("R2A", ra2.at[0:nx - 1], ra2.at[0:nx - 1], at_x(along[1]))
    r2b = copy("R2B", rb2.at[0:nx - 1], rb2.at[0:nx - 1], at_x(along[1]))
    r2c = Exchange("R2C", ny, y, at_y, lambda c: sc2.at[c], rc2.at[y], rc2.at[0:ny - 1])
    sends.extend([r2a, r2b])

    def turn_q2():
        q1.arrived()
        qy[y] = functools.reduce(jnp.add, [qx[s] for s in range(nx)])
        q2.start()

    def turn_q3():
        q2.arrived()
        qz[z] = functools.reduce(jnp.add, [qy[s] for s in range(ny)])
        q3.start()

    def turn_rc():
        r1c.arrived()
        for s in range(ny):
            sc2[s] = summed(uc[s, x], rc, x, nx, (s,)).astype(BF16)
        r2c.start()

    def row_b(k):
        sb2[k] = ended(back_b, own_b, rb, k).astype(BF16)
        if k:
            copy("R2B", sb2.at[k], rb2.at[x], at_x(along[k])).start()

    def row_a(k):
        sa2[k] = ended(back_a, own_a, ra, k).astype(BF16)
        if k:
            copy("R2A", sa2.at[k], ra2.at[x], at_x(along[k])).start()

    events = [(4.5, "turn_q2", turn_q2), (9.1, "turn_q3", turn_q3), (7.5, "turn_rc", turn_rc)]
    for i, k in enumerate(far):
        when = 3.5 + 0.7 * i
        events.append((when, f"rb{k}", functools.partial(two_off, *args_b, k)))
        events.append((when + 0.01, f"ra{k}", functools.partial(two_off, *args_a, k)))
        events.append((when + 0.02, f"nb{k}", functools.partial(next_to, *args_b, k)))
        events.append((when + 0.03, f"na{k}", functools.partial(next_to, *args_a, k)))
        when = 9.5 + 0.7 * i
        events.append((when, f"rowb{k}", functools.partial(row_b, k)))
        events.append((when + 0.01, f"rowa{k}", functools.partial(row_a, k)))
    for when, name, event in sorted(events, key=lambda e: e[0]):
        stage(name)
        event()

    stage("r2b_wait")
    r2b.wait_recv()
    stage("sum2b")
    asy[...] = summed(sb2[0], rb2, x, nx, ())
    for s in range(ny):
        s3y[s] = asy[s * rows:(s + 1) * rows, :]
    r4 = Exchange("R3Y", ny, y, at_y, lambda c: s3y.at[c], r3y.at[y], r3y.at[0:ny - 1]).start()
    stage("r2c_wait")
    r2c.arrived()
    asz[:, fa:] = summed(sc2[y], rc2, y, ny, ())
    stage("r2a_wait")
    r2a.wait_recv()
    stage("sum2")
    asz[:, :fa] = summed(sa2[0], ra2, x, nx, ())
    for s in range(nz):
        s3z[s] = asz[s * rows:(s + 1) * rows, :]
    r3 = Exchange("R3Z", nz, z, at_z, lambda c: s3z.at[c], r3z.at[z], r3z.at[0:nz - 1]).start()

    q3.arrived()
    stage("loss")
    losses = functools.reduce(jnp.add, [qz[s] for s in range(nz)]) + logs[0]
    spot = lax.broadcasted_iota(jnp.int32, (1, tokens), 1)
    for i in range(rows):
        loss[:, i:i + 1] = jnp.sum(jnp.where(spot == x * size + y * gz + z * rows + i, losses, 0.0), axis=-1, keepdims=True)

    stage("r3_wait")
    r3.arrived()
    r4.arrived()
    stage("final")
    upstream = jnp.concatenate([summed(s3z[z], r3z, z, nz, ()), summed(s3y[y], r3y, y, ny, ())], axis=-1)
    scaled = gain[...] * upstream
    inner = jnp.mean(scaled * values, axis=-1, keepdims=True)
    hd[...] = (inverse * scaled - values * (inverse * inverse * inverse) * inner).astype(BF16)

    stage("sent_wait")
    for all_sent in sends:
        all_sent.wait_send()
    other.wait_send()
    stage(None)


def finish_kernel(*refs):
    half = len(refs) // 2
    copies = [pltpu.make_async_copy(a, b, refs[-1].at[i]) for i, (a, b) in enumerate(zip(refs[:half], refs[half:-1]))]
    for copy in copies:
        copy.start()
    for copy in copies:
        copy.wait()


def finish(*arrays):
    n = len(arrays)
    return pl.pallas_call(
        finish_kernel,
        out_shape=tuple(jax.ShapeDtypeStruct(a.shape, a.dtype) for a in arrays),
        in_specs=[pl.BlockSpec(memory_space=pltpu.VMEM)] * n,
        out_specs=[pl.BlockSpec(memory_space=pl.ANY)] * n,
        scratch_shapes=[pltpu.SemaphoreType.DMA((n,))],
        compiler_params=pltpu.CompilerParams(vmem_limit_bytes=2**20),
        name="finish",
    )(*arrays)


def body(hidden, gain, head, labels):
    rows, feat = hidden.shape[1:]
    vocab = head.shape[2]
    tokens = labels.shape[0]
    ny, nx, nz = dims = GRID[tokens // rows]
    fa, fc, fb = parts = SPLIT[feat]
    fac = fa + fc
    gz, gy = nz * rows, ny * rows
    vm = pltpu.VMEM
    loss, head_grad, hidden_grad = pl.pallas_call(
        functools.partial(kernel, dims, parts),
        out_shape=(
            vm((1, rows), F32),
            vm((vocab, feat), BF16),
            vm((rows, feat), BF16),
        ),
        in_specs=[pl.BlockSpec(memory_space=pltpu.HBM)] * 4,
        out_specs=[pl.BlockSpec(memory_space=vm)] * 3,
        scratch_shapes=[
            vm((vocab, feat), BF16),
            vm((rows, feat), BF16),
            vm((nz, rows, fac), BF16),
            vm((ny, rows, fb), BF16),
            vm((gz, fac), F32),
            vm((gy, fb), F32),
            vm((ny, nx, gz, fa), BF16),
            vm((ny, nx, gz, fc), BF16),
            vm((nx, nz, gy, fb), BF16),
            vm((ny, nx, gz, fb), BF16),
            vm((nx, ny * gz, vocab), F32),
            vm((nx, ny * gz, vocab), F32),
            vm((nz, 2, tokens), F32),
            vm((ny, 2, tokens), F32),
            vm((2 * nx, 2, tokens), F32),
            vm((nx, ny * gz, 128), F32),
            vm((ny, nx, gz, 128), jnp.int32),
            vm((ny, nx, gz, vocab), BF16),
            vm((nx, nz, gy, vocab), BF16),
            vm((ny, nx, gz, fa), F32),
            vm((ny, nx, gz, fc), BF16),
            vm((nx, nz, gy, fb), F32),
            vm((ny * nx, gz, fa), BF16),
            vm((nz * nx, gy, fb), BF16),
            vm((ny * nx, gz, fa), BF16),
            vm((nx, ny, gz, fc), BF16),
            vm((nz * nx, gy, fb), BF16),
            vm((nx, gz, fa), BF16),
            vm((ny, gz, fc), BF16),
            vm((nx, gy, fb), BF16),
            vm((nx, gz, fa), BF16),
            vm((ny, gz, fc), BF16),
            vm((nx, gy, fb), BF16),
            vm((nz, rows, fac), F32),
            vm((ny, rows, fb), F32),
            vm((nz, rows, fac), F32),
            vm((ny, rows, fb), F32),
            vm((nz, 1, tokens), F32),
            vm((ny, 1, tokens), F32),
            vm((nx, 1, tokens), F32),
            pltpu.SemaphoreType.DMA((len(NUM),)),
            pltpu.SemaphoreType.DMA((len(NUM),)),
            pltpu.SemaphoreType.DMA((2, max(ny, nz) * nx)),
            pltpu.SemaphoreType.DMA((2, nx)),
            pltpu.SemaphoreType.DMA((4,)),
            vm((rows, feat), BF16),
            vm((1, feat), F32),
            vm((1, tokens), jnp.int32),
        ],
        compiler_params=pltpu.CompilerParams(collective_id=0, has_side_effects=True, vmem_limit_bytes=123 * 2**19),
        name="head_step",
    )(hidden[0], gain, head[0].T, labels.reshape(1, tokens))
    loss, head_grad, hidden_grad = finish(loss, head_grad, hidden_grad)
    return loss, head_grad.T[None], hidden_grad[None]


def solution(mesh):
    in_specs = (P("member", "fsdp", None), P("member", None), P("member", None, "fsdp"), P())
    out_specs = (P("member", "fsdp"), P("member", None, "fsdp"), P("member", "fsdp", None))
    return jax.shard_map(body, mesh=mesh, in_specs=in_specs, out_specs=out_specs, check_vma=False)
```
